256 devices in a mesh: gx: 16 (over y_lo, z), gy: 16 (over y_hi, x, core).
Axes of the slice: x: 4, y: 4 (y_hi: 2, y_lo: 2; y = y_hi * 2 + y_lo), z: 8, core: 2. Of those that a mesh axis runs over, the one named last changes fastest.
Arguments:
- phase: float32 [256, 512, 256], P('gx', 'gy'), may hold values from -1 to 1
- solute: float32 [256, 512, 256], P('gx', 'gy'), may hold values from -1 to 1
- macro_temp: float32 [64, 128, 64], P('gx', None, 'gy'), may hold values from -1 to 1
Outputs:
- phase_out: float32 [256, 512, 256], P('gx', 'gy')
- solute_out: float32 [256, 512, 256], P('gx', 'gy')
- latent_heat: float32 [64, 128, 64], P('gx', None, 'gy')
The draws below stay inside these ranges and needn't reach their ends.
All inputs are finite; a program needn't handle non-finite values.
Results may differ from the reference program's by a relative error of at most 0.0001.
Values sent between devices are 32-bit elements; how exact they have to be, the bound alone decides.
A program may use at most 64 MiB of HBM per device.

```python
import jax
import jax.numpy as jnp

NZ = 256
SUBSTEPS = 2
NX = 256
NY = 512
MX = 64
MY = 128
MZ = 64


def block_levels(stream_key, extent, shards, smallest, high):
    loudness, own = 1.0, jax.random.fold_in(stream_key, 6)
    for axis_at, parts in shards:
        draws = jnp.exp(jax.random.uniform(jax.random.fold_in(own, axis_at), (parts,), jnp.float32, smallest / len(shards), high / len(shards)))
        loudness = loudness * jnp.repeat(draws, extent[axis_at] // parts).reshape([-1 if axis == axis_at else 1 for axis in range(len(extent))])
    return loudness


def setup_inputs(seed: int = 0) -> dict:
    keys = jax.random.split(jax.random.key(seed), 4)
    phase = jnp.clip(jax.random.uniform(keys[0], (NX, NY, NZ), jnp.float32, -1.0, 1.0) * block_levels(keys[0], (NX, NY, NZ), ((0, 16), (1, 16)), -0.4, 0.0), -1.0, 1.0)
    solute = jnp.clip(jax.random.uniform(keys[1], (NX, NY, NZ), jnp.float32, -1.0, 1.0) * block_levels(keys[1], (NX, NY, NZ), ((0, 16), (1, 16)), -0.4, 0.0), -1.0, 1.0)
    macro_temp = jnp.clip(jax.random.uniform(keys[2], (MX, MY, MZ), jnp.float32, -1.0, 1.0) * block_levels(keys[2], (MX, MY, MZ), ((0, 16), (2, 16)), -0.4, 0.0), -1.0, 1.0)
    return dict(phase=phase, solute=solute, macro_temp=macro_temp)


time_step = 0.1
anisotropy = 0.3
coupling = 2.0
rejection = 0.5


def stretch(coarse, axis, count, periodic):
    size = coarse.shape[axis]
    fine = jnp.arange(count, dtype=jnp.int32)
    lower = jnp.floor_divide(2 * fine - 3, 8).astype(jnp.int32)
    frac = ((2 * fine - 3) - 8 * lower).astype(jnp.float32) / 8.0
    if periodic:
        first = (lower % size).astype(jnp.int32)
        second = ((lower + 1) % size).astype(jnp.int32)
    else:
        first = jnp.clip(lower, 0, size - 1).astype(jnp.int32)
        second = jnp.clip(lower + 1, 0, size - 1).astype(jnp.int32)
    shape = [1, 1, 1]
    shape[axis] = count
    frac = frac.reshape(shape)
    return (1.0 - frac) * jnp.take(coarse, first, axis=axis) + frac * jnp.take(coarse, second, axis=axis)


def divergence(pad_field, with_aniso):
    grid = jnp.pad(pad_field, ((0, 0), (0, 0), (2, 2)), mode="edge")
    grad_x = 0.5 * (grid[2:, 1:-1, 1:-1] - grid[:-2, 1:-1, 1:-1])
    grad_y = 0.5 * (grid[1:-1, 2:, 1:-1] - grid[1:-1, :-2, 1:-1])
    grad_z = 0.5 * (grid[1:-1, 1:-1, 2:] - grid[1:-1, 1:-1, :-2])
    if with_aniso:
        sq_x = grad_x * grad_x
        sq_y = grad_y * grad_y
        planar = sq_x + sq_y + 1.0
        factor = 1.0 + anisotropy * (sq_x * sq_x - 6.0 * sq_x * sq_y + sq_y * sq_y) / (planar * planar)
        stiff = factor * factor
        grad_x = stiff * grad_x
        grad_y = stiff * grad_y
        grad_z = stiff * grad_z
    total = 0.5 * (grad_x[2:, 1:-1, 1:-1] - grad_x[:-2, 1:-1, 1:-1])
    total = total + 0.5 * (grad_y[1:-1, 2:, 1:-1] - grad_y[1:-1, :-2, 1:-1])
    total = total + 0.5 * (grad_z[1:-1, 1:-1, 2:] - grad_z[1:-1, 1:-1, :-2])
    return total


def substep(phase_pad, solute_pad, theta):
    old = phase_pad[2:-2, 2:-2, :]
    conc = solute_pad[2:-2, 2:-2, :]
    square = 1.0 - old * old
    drive = divergence(phase_pad, True) + old - old * old * old - coupling * square * square * (theta + conc)
    new_phase = old + time_step * drive
    new_solute = conc + time_step * divergence(solute_pad, False) + rejection * (new_phase - old)
    return new_phase, new_solute


def reference(phase, solute, macro_temp):
    theta = stretch(macro_temp, 0, NX, True)
    theta = stretch(theta, 1, NY, True)
    theta = stretch(theta, 2, NZ, False)
    current_phase, current_solute = phase, solute
    for step in range(SUBSTEPS):
        phase_pad = jnp.pad(current_phase, ((2, 2), (2, 2), (0, 0)), mode="wrap")
        solute_pad = jnp.pad(current_solute, ((2, 2), (2, 2), (0, 0)), mode="wrap")
        current_phase, current_solute = substep(phase_pad, solute_pad, theta)
    change = 0.5 * (current_phase - phase)
    latent = change.reshape(MX, 4, MY, 4, MZ, 4).mean(axis=(1, 3, 5))
    return current_phase, current_solute, latent
```

```python
import functools

import jax
import jax.numpy as jnp
import numpy as np
from jax import lax
from jax.experimental import pallas as pl
from jax.experimental.pallas import tpu as pltpu
from jax.sharding import PartitionSpec as P

MESH = pl.DeviceIdType.MESH
HIGHEST = lax.Precision.HIGHEST

BX, BY = 16, 32
M = 4
EX = BX + 2 * M
RY = 8
EY = 48
LANES = 128
ROWS = (4, 12, 20, 28, 36)
OWN = (8, 16, 24, 32)


def tables(parts):
    wy = np.zeros((128, 4 * LANES), np.float32)
    for row in range(40):
        y = row - 4
        low = (2 * y - 3) // 8
        frac = (2 * y - 3 - 8 * low) / 8.0
        for hit, weight in ((low + 1, 1.0 - frac), (low + 2, frac)):
            if 0 <= hit < 10:
                for z in range(4):
                    wy[32 * z + hit, LANES * z + row] += weight
    wz = np.zeros((64, 256), np.float32)
    for fine in range(256):
        low = (2 * fine - 3) // 8
        frac = (2 * fine - 3 - 8 * low) / 8.0
        for hit, weight in ((low, 1.0 - frac), (low + 1, frac)):
            hit = min(max(hit, 0), 63)
            wz[16 * (hit % 4) + hit // 4, fine] += weight
    py = np.zeros((32, 32), np.float32)
    for y in range(32):
        py[y // 4, y] = 1.0
    pz = np.zeros((64, 256), np.float32)
    for fine in range(256):
        z = fine // 4
        pz[16 * (z % 4) + z // 4, fine] = 1.0 / 128.0
    return wy, wz, py, pz


def kernel(nx, ny, p_in, c_in, m_in, wy_in, wz_in, py_in, pz_in, p_out, c_out, lat_out,
           p0, c0, p1, c1, fx, fy, fz, th, p2, c2, lat, wy, wz, py, pz, mac, s1, r1, xs, xr, s2, r2, lat_v,
           load_sem, out_sem, x_send, x_recv, y_send, y_recv, d_send, d_recv, t_send, t_recv, h_send, h_recv, l_send, l_recv):
    a = lax.axis_index("gx")
    b = lax.axis_index("gy")
    up_x, down_x = lax.rem(a + 1, nx), lax.rem(a + nx - 1, nx)
    up_y, down_y = lax.rem(b + 1, ny), lax.rem(b + ny - 1, ny)

    own = slice(M, M + BX)
    loads = []
    for f, (src, dst) in enumerate(((p_in, p0), (c_in, c0))):
        for h in range(2):
            loads.append(pltpu.make_async_copy(
                src.at[:, :, pl.ds(h * LANES, LANES)],
                dst.at[h, pl.ds(M, BX), pl.ds(RY, BY), :],
                load_sem.at[2 * f + h]))
    for k, (src, dst) in enumerate(((m_in, mac), (wy_in, wy), (wz_in, wz), (py_in, py), (pz_in, pz))):
        loads.append(pltpu.make_async_copy(src, dst, load_sem.at[4 + k]))
    loads[4].start()
    for copy in loads[:4] + loads[5:]:
        copy.start()

    barrier = pltpu.get_barrier_semaphore()
    corners = ((up_x, up_y), (up_x, down_y), (down_x, up_y), (down_x, down_y))
    peers = [(up_x, b), (down_x, b)] + list(corners)
    for k in range(1, ny):
        peers.append((a, lax.rem(b + k, ny)))
    for peer in peers:
        pl.semaphore_signal(barrier, inc=1, device_id=peer, device_id_type=MESH)

    lane = lax.broadcasted_iota(jnp.int32, (8, LANES), 1)
    first, last = lane == 0, lane == LANES - 1
    first2, last2 = lane < 2, lane >= LANES - 2

    loads[4].wait()
    lane4 = lax.broadcasted_iota(jnp.int32, (4, LANES), 1)
    zone = lane4 // 32
    layers = [mac[pl.ds(z, 4, stride=4), :] for z in range(4)]
    for dest in range(16):
        parts = [pltpu.roll(layers[z], (32 * z - 8 * dest + 1) % LANES, 1) for z in range(4)]
        tile = jnp.where(zone == 0, parts[0], jnp.where(zone == 1, parts[1], jnp.where(zone == 2, parts[2], parts[3])))
        s1[pl.ds(8 * dest, 4), :] = tile

    for copy in loads[:4]:
        copy.wait()
    pl.semaphore_wait(barrier, len(peers))

    x_copies, y_copies, d_copies = [], [], []
    lo, hi = pl.ds(M, M), pl.ds(BX, M)
    before, after = pl.ds(0, M), pl.ds(M + BX, M)
    row_lo, row_hi = pl.ds(RY, M), pl.ds(RY + BY - M, M)
    row_before, row_after = pl.ds(RY - M, M), pl.ds(RY + BY, M)
    rows, planes = pl.ds(RY, BY), pl.ds(M, BX)

    def remote(src, dst, send, recv, peer):
        return pltpu.make_async_remote_copy(
            src_ref=src, dst_ref=dst, send_sem=send, recv_sem=recv, device_id=peer, device_id_type=MESH)

    for f, field in enumerate((p0, c0)):
        for side, (src, dst, peer) in enumerate(((hi, before, (up_x, b)), (lo, after, (down_x, b)))):
            k = 2 * f + side
            x_copies.append(remote(field.at[:, src, rows, :], field.at[:, dst, rows, :], x_send.at[k], x_recv.at[k], peer))
        for side, (src, dst, peer) in enumerate(((row_hi, row_before, (a, up_y)), (row_lo, row_after, (a, down_y)))):
            k = 2 * f + side
            y_copies.append(remote(field.at[:, planes, src, :], field.at[:, planes, dst, :], y_send.at[k], y_recv.at[k], peer))
        for side, (sx, dx, sy, dy, peer) in enumerate((
            (hi, before, row_hi, row_before, corners[0]),
            (hi, before, row_lo, row_after, corners[1]),
            (lo, after, row_hi, row_before, corners[2]),
            (lo, after, row_lo, row_after, corners[3]),
        )):
            k = 4 * f + side
            d_copies.append(remote(field.at[:, sx, sy, :], field.at[:, dx, dy, :], d_send.at[k], d_recv.at[k], peer))
    for copy in x_copies + y_copies:
        copy.start()

    def exchange(src, dst, send, recv):
        out = []
        for k in range(1, ny):
            to = lax.rem(b + k, ny)
            out.append(remote(
                src.at[pl.ds(pl.multiple_of(8 * to, 8), 8), :], dst.at[pl.ds(pl.multiple_of(8 * b, 8), 8), :],
                send.at[k], recv.at[k], (a, to)))
        return out

    here = pl.ds(pl.multiple_of(8 * b, 8), 8)
    t_copies = exchange(s1, r1, t_send, t_recv)
    for copy in t_copies:
        copy.start()
    for copy in d_copies:
        copy.start()
    r1[here, :] = s1[here, :]
    for copy in t_copies:
        copy.wait_recv()
    xs[0] = r1[pl.ds(3, 16, stride=8), :]
    xs[1] = r1[pl.ds(0, 16, stride=8), :]
    h_copies = [remote(xs.at[0], xr.at[0], h_send.at[0], h_recv.at[0], (up_x, b)),
                remote(xs.at[1], xr.at[1], h_send.at[1], h_recv.at[1], (down_x, b))]
    for copy in h_copies:
        copy.start()

    def flux(p, e):
        for r in ROWS:
            at = pl.ds(r, 8)
            v = [p[h, e, at, :] for h in range(2)]
            fwd = [pltpu.roll(v[h], 1, 1) for h in range(2)]
            bwd = [pltpu.roll(v[h], LANES - 1, 1) for h in range(2)]
            gz = [jnp.where(last, bwd[1], bwd[0]) - jnp.where(first, v[0], fwd[0]),
                  jnp.where(last, v[1], bwd[1]) - jnp.where(first, fwd[0], fwd[1])]
            wz_ = []
            for h in range(2):
                gx = p[h, e + 1, at, :] - p[h, e - 1, at, :]
                gy = p[h, e, pl.ds(r + 1, 8), :] - p[h, e, pl.ds(r - 1, 8), :]
                sx, sy = gx * gx, gy * gy
                total = sx + sy
                planar = total + 4.0
                ratio = (total * total - 8.0 * (sx * sy)) / (planar * planar)
                factor = 1.0 + 0.3 * ratio
                stiff = factor * factor
                fx[h, e, at, :] = stiff * gx
                fy[h, e, at, :] = stiff * gy
                wz_.append(stiff * gz[h])
            fwd = [pltpu.roll(w, 1, 1) for w in wz_]
            bwd = [pltpu.roll(w, LANES - 1, 1) for w in wz_]
            fz[0, e, at, :] = jnp.where(last, bwd[1], bwd[0]) - jnp.where(first, 0.0, fwd[0])
            fz[1, e, at, :] = jnp.where(last, 0.0, bwd[1]) - jnp.where(first, fwd[0], fwd[1])

    def update(p, c, e, r, theta, store):
        at = pl.ds(r, 8)
        v = [c[h, e, at, :] for h in range(2)]
        fwd = [pltpu.roll(v[h], 2, 1) for h in range(2)]
        bwd = [pltpu.roll(v[h], LANES - 2, 1) for h in range(2)]
        head = jnp.where(first, v[0], pltpu.roll(v[0], 1, 1))
        tail = jnp.where(last, v[1], pltpu.roll(v[1], LANES - 1, 1))
        lz = [jnp.where(last2, bwd[1], bwd[0]) + jnp.where(first2, head, fwd[0]),
              jnp.where(last2, tail, bwd[1]) + jnp.where(first2, fwd[0], fwd[1])]
        for h in range(2):
            div = (fx[h, e + 1, at, :] - fx[h, e - 1, at, :]
                   + (fy[h, e, pl.ds(r + 1, 8), :] - fy[h, e, pl.ds(r - 1, 8), :]) + fz[h, e, at, :])
            old = p[h, e, at, :]
            conc = v[h]
            square = 1.0 - old * old
            step = square * (0.1 * old - 0.2 * (square * (theta[h] + conc))) + 0.025 * div
            lap = (c[h, e + 2, at, :] + c[h, e - 2, at, :]
                   + (c[h, e, pl.ds(r + 2, 8), :] + c[h, e, pl.ds(r - 2, 8), :]) + lz[h])
            store(h, old + step, conc + (0.025 * (lap - 6.0 * conc) + 0.5 * step))

    def flux_pair(p, start, gap, at_gap):
        def run(i, carry):
            e = start + 2 * i + jnp.where(i >= at_gap, gap, 0)
            flux(p, e)
            flux(p, e + 1)
            return carry
        return run

    def first_update(group):
        e0 = 4 * group + 2
        for r in ROWS:
            at = pl.ds(r, 8)
            low = [th[group, h, at, :] for h in range(2)]
            rise = [th[group + 1, h, at, :] - low[h] for h in range(2)]
            for q in range(4):
                theta = [low[h] + (0.125 + 0.25 * q) * rise[h] for h in range(2)]
                def store(h, new_p, new_c):
                    p1[h, e0 + q, at, :] = new_p
                    c1[h, e0 + q, at, :] = new_c
                update(p0, c0, e0 + q, r, theta, store)

    def second_update(group):
        e0 = 4 * group + 4
        for r in OWN:
            at = pl.ds(r, 8)
            to = pl.ds(r - RY, 8)
            total = [None, None]
            for q in range(4):
                low = [th[group + q // 2, h, at, :] for h in range(2)]
                rise = [th[group + q // 2 + 1, h, at, :] - low[h] for h in range(2)]
                frac = 0.125 + 0.25 * ((q + 2) % 4)
                theta = [low[h] + frac * rise[h] for h in range(2)]
                def store(h, new_p, new_c):
                    p2[h, e0 + q - M, to, :] = new_p
                    c2[h, e0 + q - M, to, :] = new_c
                    change = new_p - p0[h, e0 + q, at, :]
                    total[h] = change if total[h] is None else total[h] + change
                update(p1, c1, e0 + q, r, theta, store)
            for h in range(2):
                lat[group, to, pl.ds(h * LANES, LANES)] = total[h]

    for copy in y_copies:
        copy.wait_recv()
    lax.fori_loop(0, 7, flux_pair(p0, 5, 0, 99), 0)

    for copy in loads[5:]:
        copy.wait()
    for copy in h_copies:
        copy.wait_recv()
    coarse = [xr[0]] + [r1[pl.ds(x, 16, stride=8), :] for x in range(4)] + [xr[1]]
    on_rows = jnp.dot(jnp.concatenate(coarse, axis=0), wy[...], precision=HIGHEST, preferred_element_type=jnp.float32)
    for x in range(6):
        part = jnp.concatenate([on_rows[16 * x:16 * x + 16, LANES * z:LANES * z + LANES] for z in range(4)], axis=0)
        full = lax.dot_general(part, wz[...], (((0,), (0,)), ((), ())), precision=HIGHEST, preferred_element_type=jnp.float32)
        for h in range(2):
            th[x, h, pl.ds(4, 40), :] = full[:40, LANES * h:LANES * h + LANES]

    lax.fori_loop(1, 4, lambda i, carry: (first_update(i), carry)[1], 0)
    lax.fori_loop(0, 5, flux_pair(p1, 7, 0, 99), 0)
    lax.fori_loop(1, 3, lambda i, carry: (second_update(i), carry)[1], 0)

    def results(k, start, count):
        out = []
        for f, (src, dst) in enumerate(((p2, p_out), (c2, c_out))):
            for h in range(2):
                out.append(pltpu.make_async_copy(
                    src.at[h, pl.ds(start, count), :, :],
                    dst.at[pl.ds(start, count), :, pl.ds(h * LANES, LANES)],
                    out_sem.at[4 * k + 2 * f + h]))
        return out

    outs = results(0, 4, 8)
    for copy in outs:
        copy.start()

    for copy in x_copies + d_copies:
        copy.wait_recv()
    lax.fori_loop(0, 4, flux_pair(p0, 1, 14, 2), 0)
    lax.fori_loop(0, 2, lambda i, carry: (first_update(4 * i), carry)[1], 0)
    lax.fori_loop(0, 4, flux_pair(p1, 3, 10, 2), 0)
    lax.fori_loop(0, 2, lambda i, carry: (second_update(3 * i), carry)[1], 0)
    more = results(1, 0, 4) + results(2, 12, 4)
    for copy in more:
        copy.start()

    for x in range(4):
        on_y = jnp.dot(py[...], lat[x], precision=HIGHEST, preferred_element_type=jnp.float32)
        on_z = lax.dot_general(pz[...], on_y, (((1,), (1,)), ((), ())), precision=HIGHEST, preferred_element_type=jnp.float32)
        s2[pl.ds(x, 16, stride=8), :] = jnp.concatenate([on_z[16 * z:16 * z + 16] for z in range(4)], axis=1)
    l_copies = exchange(s2, r2, l_send, l_recv)
    for copy in l_copies:
        copy.start()
    r2[here, :] = s2[here, :]
    for copy in l_copies:
        copy.wait_recv()
    block = lane4 // 8
    for z in range(4):
        row = None
        for s in range(16):
            part = pltpu.roll(r2[pl.ds(8 * s, 4), :], (8 * s - 32 * z) % LANES, 1)
            row = part if row is None else jnp.where(block == s, part, row)
        lat_v[pl.ds(z, 4, stride=4), :] = row
    final = pltpu.make_async_copy(lat_v, lat_out, out_sem.at[12])
    final.start()

    for copy in x_copies + y_copies + d_copies + t_copies + h_copies + l_copies:
        copy.wait_send()
    for copy in outs + more:
        copy.wait()
    final.wait()


def body(nx, ny, phase, solute, macro_temp):
    macro = jnp.transpose(macro_temp, (0, 2, 1)).reshape(16, LANES)
    wy, wz, py, pz = (jnp.asarray(t) for t in tables(ny))
    f32 = jnp.float32
    anywhere = pl.BlockSpec(memory_space=pl.ANY)
    wide = pltpu.VMEM((2, EX, EY, LANES), f32)
    dma = pltpu.SemaphoreType.DMA
    new_phase, new_solute, latent = pl.pallas_call(
        functools.partial(kernel, nx, ny),
        out_shape=(jax.ShapeDtypeStruct(phase.shape, f32), jax.ShapeDtypeStruct(solute.shape, f32),
                   jax.ShapeDtypeStruct((16, LANES), f32)),
        in_specs=[anywhere] * 7,
        out_specs=(anywhere,) * 3,
        scratch_shapes=[wide] * 7 + [
            pltpu.VMEM((6, 2, EY, LANES), f32),
            pltpu.VMEM((2, BX, BY, LANES), f32), pltpu.VMEM((2, BX, BY, LANES), f32),
            pltpu.VMEM((4, BY, 2 * LANES), f32),
            pltpu.VMEM(wy.shape, f32), pltpu.VMEM(wz.shape, f32), pltpu.VMEM(py.shape, f32), pltpu.VMEM(pz.shape, f32),
            pltpu.VMEM((16, LANES), f32),
            pltpu.VMEM((128, LANES), f32), pltpu.VMEM((128, LANES), f32),
            pltpu.VMEM((2, 16, LANES), f32), pltpu.VMEM((2, 16, LANES), f32),
            pltpu.VMEM((128, LANES), f32), pltpu.VMEM((128, LANES), f32),
            pltpu.VMEM((16, LANES), f32),
            dma((9,)), dma((13,)), dma((4,)), dma((4,)), dma((4,)), dma((4,)), dma((8,)), dma((8,)),
            dma((16,)), dma((16,)), dma((2,)), dma((2,)), dma((16,)), dma((16,)),
        ],
        compiler_params=pltpu.CompilerParams(collective_id=0, has_side_effects=True, vmem_limit_bytes=40 << 20),
        name="substeps",
    )(phase, solute, macro, wy, wz, py, pz)
    return new_phase, new_solute, jnp.transpose(latent.reshape(4, 4, LANES), (0, 2, 1))


def solution(mesh):
    in_specs = (P("gx", "gy", None), P("gx", "gy", None), P("gx", None, "gy"))
    out_specs = (P("gx", "gy", None), P("gx", "gy", None), P("gx", None, "gy"))
    return jax.shard_map(
        functools.partial(body, mesh.shape["gx"], mesh.shape["gy"]),
        mesh=mesh, in_specs=in_specs, out_specs=out_specs, check_vma=False)
```

```python
import functools

import jax
import jax.numpy as jnp
import numpy as np
from jax import lax
from jax.experimental import pallas as pl
from jax.experimental.pallas import tpu as pltpu
from jax.sharding import PartitionSpec as P

MESH = pl.DeviceIdType.MESH
HIGHEST = lax.Precision.HIGHEST

BX, BY = 16, 32
M = 4
EX = BX + 2 * M
RY = 8
EY = 48
LANES = 128
ROWS = (4, 12, 20, 28, 36)
OWN = (8, 16, 24, 32)


def tables(parts):
    wy = np.zeros((128, 4 * LANES), np.float32)
    for row in range(40):
        y = row - 4
        low = (2 * y - 3) // 8
        frac = (2 * y - 3 - 8 * low) / 8.0
        for hit, weight in ((low + 1, 1.0 - frac), (low + 2, frac)):
            if 0 <= hit < 10:
                for z in range(4):
                    wy[32 * z + hit, LANES * z + row] += weight
    wz = np.zeros((64, 256), np.float32)
    for fine in range(256):
        low = (2 * fine - 3) // 8
        frac = (2 * fine - 3 - 8 * low) / 8.0
        for hit, weight in ((low, 1.0 - frac), (low + 1, frac)):
            hit = min(max(hit, 0), 63)
            wz[16 * (hit % 4) + hit // 4, fine] += weight
    py = np.zeros((32, 32), np.float32)
    for y in range(32):
        py[y // 4, y] = 1.0
    pz = np.zeros((64, 256), np.float32)
    for fine in range(256):
        z = fine // 4
        pz[16 * (z % 4) + z // 4, fine] = 1.0 / 128.0
    return wy, wz, py, pz


def kernel(nx, ny, p_in, c_in, m_in, wy_in, wz_in, py_in, pz_in, p_out, c_out, lat_out,
           p0, c0, p1, c1, fx, fy, fz, th, p2, c2, lat, wy, wz, py, pz, mac, s1, r1, xs, xr, s2, r2, lat_v,
           load_sem, out_sem, x_send, x_recv, y_send, y_recv, d_send, d_recv, t_send, t_recv, h_send, h_recv, l_send, l_recv):
    a = lax.axis_index("gx")
    b = lax.axis_index("gy")
    up_x, down_x = lax.rem(a + 1, nx), lax.rem(a + nx - 1, nx)
    up_y, down_y = lax.rem(b + 1, ny), lax.rem(b + ny - 1, ny)

    own = slice(M, M + BX)
    loads = []
    for f, (src, dst) in enumerate(((p_in, p0), (c_in, c0))):
        for h in range(2):
            loads.append(pltpu.make_async_copy(
                src.at[:, :, pl.ds(h * LANES, LANES)],
                dst.at[h, pl.ds(M, BX), pl.ds(RY, BY), :],
                load_sem.at[2 * f + h]))
    for k, (src, dst) in enumerate(((m_in, mac), (wy_in, wy), (wz_in, wz), (py_in, py), (pz_in, pz))):
        loads.append(pltpu.make_async_copy(src, dst, load_sem.at[4 + k]))
    loads[4].start()
    for copy in loads[:4] + loads[5:]:
        copy.start()

    barrier = pltpu.get_barrier_semaphore()
    corners = ((up_x, up_y), (up_x, down_y), (down_x, up_y), (down_x, down_y))
    peers = [(up_x, b), (down_x, b)] + list(corners)
    for k in range(1, ny):
        peers.append((a, lax.rem(b + k, ny)))
    for peer in peers:
        pl.semaphore_signal(barrier, inc=1, device_id=peer, device_id_type=MESH)

    lane = lax.broadcasted_iota(jnp.int32, (8, LANES), 1)
    first, last = lane == 0, lane == LANES - 1
    first2, last2 = lane < 2, lane >= LANES - 2

    loads[4].wait()
    lane4 = lax.broadcasted_iota(jnp.int32, (4, LANES), 1)
    zone = lane4 // 32
    layers = [mac[pl.ds(z, 4, stride=4), :] for z in range(4)]
    for dest in range(16):
        parts = [pltpu.roll(layers[z], (32 * z - 8 * dest + 1) % LANES, 1) for z in range(4)]
        tile = jnp.where(zone == 0, parts[0], jnp.where(zone == 1, parts[1], jnp.where(zone == 2, parts[2], parts[3])))
        s1[pl.ds(8 * dest, 4), :] = tile

    for copy in loads[:4]:
        copy.wait()
    pl.semaphore_wait(barrier, len(peers))

    x_copies, y_copies, d_copies = [], [], []
    lo, hi = pl.ds(M, M), pl.ds(BX, M)
    before, after = pl.ds(0, M), pl.ds(M + BX, M)
    row_lo, row_hi = pl.ds(RY, M), pl.ds(RY + BY - M, M)
    row_before, row_after = pl.ds(RY - M, M), pl.ds(RY + BY, M)
    rows, planes = pl.ds(RY, BY), pl.ds(M, BX)

    def remote(src, dst, send, recv, peer):
        return pltpu.make_async_remote_copy(
            src_ref=src, dst_ref=dst, send_sem=send, recv_sem=recv, device_id=peer, device_id_type=MESH)

    for f, field in enumerate((p0, c0)):
        for side, (src, dst, peer) in enumerate(((hi, before, (up_x, b)), (lo, after, (down_x, b)))):
            k = 2 * f + side
            x_copies.append(remote(field.at[:, src, rows, :], field.at[:, dst, rows, :], x_send.at[k], x_recv.at[k], peer))
        for side, (src, dst, peer) in enumerate(((row_hi, row_before, (a, up_y)), (row_lo, row_after, (a, down_y)))):
            k = 2 * f + side
            y_copies.append(remote(field.at[:, planes, src, :], field.at[:, planes, dst, :], y_send.at[k], y_recv.at[k], peer))
        for side, (sx, dx, sy, dy, peer) in enumerate((
            (hi, before, row_hi, row_before, corners[0]),
            (hi, before, row_lo, row_after, corners[1]),
            (lo, after, row_hi, row_before, corners[2]),
            (lo, after, row_lo, row_after, corners[3]),
        )):
            k = 4 * f + side
            d_copies.append(remote(field.at[:, sx, sy, :], field.at[:, dx, dy, :], d_send.at[k], d_recv.at[k], peer))
    for copy in x_copies + y_copies:
        copy.start()

    def exchange(src, dst, send, recv):
        out = []
        for k in range(1, ny):
            to = lax.rem(b + k, ny)
            out.append(remote(
                src.at[pl.ds(pl.multiple_of(8 * to, 8), 8), :], dst.at[pl.ds(pl.multiple_of(8 * b, 8), 8), :],
                send.at[k], recv.at[k], (a, to)))
        return out

    here = pl.ds(pl.multiple_of(8 * b, 8), 8)
    t_copies = exchange(s1, r1, t_send, t_recv)
    for copy in t_copies:
        copy.start()
    for copy in d_copies:
        copy.start()
    r1[here, :] = s1[here, :]
    for copy in t_copies:
        copy.wait_recv()
    xs[0] = r1[pl.ds(3, 16, stride=8), :]
    xs[1] = r1[pl.ds(0, 16, stride=8), :]
    h_copies = [remote(xs.at[0], xr.at[0], h_send.at[0], h_recv.at[0], (up_x, b)),
                remote(xs.at[1], xr.at[1], h_send.at[1], h_recv.at[1], (down_x, b))]
    for copy in h_copies:
        copy.start()

    def flux(p, e):
        for r in ROWS:
            at = pl.ds(r, 8)
            v = [p[h, e, at, :] for h in range(2)]
            fwd = [pltpu.roll(v[h], 1, 1) for h in range(2)]
            bwd = [pltpu.roll(v[h], LANES - 1, 1) for h in range(2)]
            gz = [jnp.where(last, bwd[1], bwd[0]) - jnp.where(first, v[0], fwd[0]),
                  jnp.where(last, v[1], bwd[1]) - jnp.where(first, fwd[0], fwd[1])]
            wz_ = []
            for h in range(2):
                gx = p[h, e + 1, at, :] - p[h, e - 1, at, :]
                gy = p[h, e, pl.ds(r + 1, 8), :] - p[h, e, pl.ds(r - 1, 8), :]
                sx, sy = gx * gx, gy * gy
                total = sx + sy
                planar = total + 4.0
                ratio = (total * total - 8.0 * (sx * sy)) / (planar * planar)
                factor = 1.0 + 0.3 * ratio
                stiff = factor * factor
                fx[h, e, at, :] = stiff * gx
                fy[h, e, at, :] = stiff * gy
                wz_.append(stiff * gz[h])
            fwd = [pltpu.roll(w, 1, 1) for w in wz_]
            bwd = [pltpu.roll(w, LANES - 1, 1) for w in wz_]
            fz[0, e, at, :] = jnp.where(last, bwd[1], bwd[0]) - jnp.where(first, 0.0, fwd[0])
            fz[1, e, at, :] = jnp.where(last, 0.0, bwd[1]) - jnp.where(first, fwd[0], fwd[1])

    def update(p, c, e, r, theta, store):
        at = pl.ds(r, 8)
        v = [c[h, e, at, :] for h in range(2)]
        fwd = [pltpu.roll(v[h], 2, 1) for h in range(2)]
        bwd = [pltpu.roll(v[h], LANES - 2, 1) for h in range(2)]
        head = jnp.where(first, v[0], pltpu.roll(v[0], 1, 1))
        tail = jnp.where(last, v[1], pltpu.roll(v[1], LANES - 1, 1))
        lz = [jnp.where(last2, bwd[1], bwd[0]) + jnp.where(first2, head, fwd[0]),
              jnp.where(last2, tail, bwd[1]) + jnp.where(first2, fwd[0], fwd[1])]
        for h in range(2):
            div = (fx[h, e + 1, at, :] - fx[h, e - 1, at, :]
                   + (fy[h, e, pl.ds(r + 1, 8), :] - fy[h, e, pl.ds(r - 1, 8), :]) + fz[h, e, at, :])
            old = p[h, e, at, :]
            conc = v[h]
            square = 1.0 - old * old
            step = square * (0.1 * old - 0.2 * (square * (theta[h] + conc))) + 0.025 * div
            lap = (c[h, e + 2, at, :] + c[h, e - 2, at, :]
                   + (c[h, e, pl.ds(r + 2, 8), :] + c[h, e, pl.ds(r - 2, 8), :]) + lz[h])
            store(h, old + step, conc + (0.025 * (lap - 6.0 * conc) + 0.5 * step))

    def flux_pair(p, start, gap, at_gap):
        def run(i, carry):
            e = start + 2 * i + jnp.where(i >= at_gap, gap, 0)
            flux(p, e)
            flux(p, e + 1)
            return carry
        return run

    def first_update(group):
        e0 = 4 * group + 2
        for r in ROWS:
            at = pl.ds(r, 8)
            low = [th[group, h, at, :] for h in range(2)]
            rise = [th[group + 1, h, at, :] - low[h] for h in range(2)]
            for q in range(4):
                theta = [low[h] + (0.125 + 0.25 * q) * rise[h] for h in range(2)]
                def store(h, new_p, new_c):
                    p1[h, e0 + q, at, :] = new_p
                    c1[h, e0 + q, at, :] = new_c
                update(p0, c0, e0 + q, r, theta, store)

    def second_update(group):
        e0 = 4 * group + 4
        for r in OWN:
            at = pl.ds(r, 8)
            to = pl.ds(r - RY, 8)
            total = [None, None]
            for q in range(4):
                low = [th[group + q // 2, h, at, :] for h in range(2)]
                rise = [th[group + q // 2 + 1, h, at, :] - low[h] for h in range(2)]
                frac = 0.125 + 0.25 * ((q + 2) % 4)
                theta = [low[h] + frac * rise[h] for h in range(2)]
                def store(h, new_p, new_c):
                    p2[h, e0 + q - M, to, :] = new_p
                    c2[h, e0 + q - M, to, :] = new_c
                    change = new_p - p0[h, e0 + q, at, :]
                    total[h] = change if total[h] is None else total[h] + change
                update(p1, c1, e0 + q, r, theta, store)
            for h in range(2):
                lat[group, to, pl.ds(h * LANES, LANES)] = total[h]

    for copy in y_copies:
        copy.wait_recv()
    lax.fori_loop(0, 7, flux_pair(p0, 5, 0, 99), 0)

    for copy in loads[5:]:
        copy.wait()
    for copy in h_copies:
        copy.wait_recv()
    coarse = [xr[0]] + [r1[pl.ds(x, 16, stride=8), :] for x in range(4)] + [xr[1]]
    on_rows = jnp.dot(jnp.concatenate(coarse, axis=0), wy[...], precision=HIGHEST, preferred_element_type=jnp.float32)
    for x in range(6):
        part = jnp.concatenate([on_rows[16 * x:16 * x + 16, LANES * z:LANES * z + LANES] for z in range(4)], axis=0)
        full = lax.dot_general(part, wz[...], (((0,), (0,)), ((), ())), precision=HIGHEST, preferred_element_type=jnp.float32)
        for h in range(2):
            th[x, h, pl.ds(4, 40), :] = full[:40, LANES * h:LANES * h + LANES]

    lax.fori_loop(1, 4, lambda i, carry: (first_update(i), carry)[1], 0)
    lax.fori_loop(0, 5, flux_pair(p1, 7, 0, 99), 0)
    lax.fori_loop(1, 3, lambda i, carry: (second_update(i), carry)[1], 0)

    def results(k, start, count):
        out = []
        for f, (src, dst) in enumerate(((p2, p_out), (c2, c_out))):
            for h in range(2):
                out.append(pltpu.make_async_copy(
                    src.at[h, pl.ds(start, count), :, :],
                    dst.at[pl.ds(start, count), :, pl.ds(h * LANES, LANES)],
                    out_sem.at[4 * k + 2 * f + h]))
        return out

    outs = results(0, 4, 8)
    for copy in outs:
        copy.start()

    for copy in x_copies + d_copies:
        copy.wait_recv()
    lax.fori_loop(0, 4, flux_pair(p0, 1, 14, 2), 0)
    lax.fori_loop(0, 2, lambda i, carry: (first_update(4 * i), carry)[1], 0)
    lax.fori_loop(0, 4, flux_pair(p1, 3, 10, 2), 0)
    lax.fori_loop(0, 2, lambda i, carry: (second_update(3 * i), carry)[1], 0)
    more = results(1, 0, 4) + results(2, 12, 4)
    for copy in more:
        copy.start()

    for x in range(4):
        on_y = jnp.dot(py[...], lat[x], precision=HIGHEST, preferred_element_type=jnp.float32)
        on_z = lax.dot_general(pz[...], on_y, (((1,), (1,)), ((), ())), precision=HIGHEST, preferred_element_type=jnp.float32)
        s2[pl.ds(x, 16, stride=8), :] = jnp.concatenate([on_z[16 * z:16 * z + 16] for z in range(4)], axis=1)
    l_copies = exchange(s2, r2, l_send, l_recv)
    for copy in l_copies:
        copy.start()
    r2[here, :] = s2[here, :]
    for copy in l_copies:
        copy.wait_recv()
    block = lane4 // 8
    for z in range(4):
        row = None
        for s in range(16):
            part = pltpu.roll(r2[pl.ds(8 * s, 4), :], (8 * s - 32 * z) % LANES, 1)
            row = part if row is None else jnp.where(block == s, part, row)
        lat_v[pl.ds(z, 4, stride=4), :] = row
    final = pltpu.make_async_copy(lat_v, lat_out, out_sem.at[12])
    final.start()

    for copy in x_copies + y_copies + d_copies + t_copies + h_copies + l_copies:
        copy.wait_send()
    for copy in outs + more:
        copy.wait()
    final.wait()


def body(nx, ny, phase, solute, macro_temp):
    macro = jnp.transpose(macro_temp, (0, 2, 1)).reshape(16, LANES)
    wy, wz, py, pz = (jnp.asarray(t) for t in tables(ny))
    f32 = jnp.float32
    anywhere = pl.BlockSpec(memory_space=pltpu.HBM)
    wide = pltpu.VMEM((2, EX, EY, LANES), f32)
    dma = pltpu.SemaphoreType.DMA
    new_phase, new_solute, latent = pl.pallas_call(
        functools.partial(kernel, nx, ny),
        out_shape=(jax.ShapeDtypeStruct(phase.shape, f32), jax.ShapeDtypeStruct(solute.shape, f32),
                   jax.ShapeDtypeStruct((16, LANES), f32)),
        in_specs=[anywhere] * 7,
        out_specs=(anywhere,) * 3,
        scratch_shapes=[wide] * 7 + [
            pltpu.VMEM((6, 2, EY, LANES), f32),
            pltpu.VMEM((2, BX, BY, LANES), f32), pltpu.VMEM((2, BX, BY, LANES), f32),
            pltpu.VMEM((4, BY, 2 * LANES), f32),
            pltpu.VMEM(wy.shape, f32), pltpu.VMEM(wz.shape, f32), pltpu.VMEM(py.shape, f32), pltpu.VMEM(pz.shape, f32),
            pltpu.VMEM((16, LANES), f32),
            pltpu.VMEM((128, LANES), f32), pltpu.VMEM((128, LANES), f32),
            pltpu.VMEM((2, 16, LANES), f32), pltpu.VMEM((2, 16, LANES), f32),
            pltpu.VMEM((128, LANES), f32), pltpu.VMEM((128, LANES), f32),
            pltpu.VMEM((16, LANES), f32),
            dma((9,)), dma((13,)), dma((4,)), dma((4,)), dma((4,)), dma((4,)), dma((8,)), dma((8,)),
            dma((16,)), dma((16,)), dma((2,)), dma((2,)), dma((16,)), dma((16,)),
        ],
        compiler_params=pltpu.CompilerParams(collective_id=0, has_side_effects=True, vmem_limit_bytes=60 << 20),
        name="substeps",
    )(phase, solute, macro, wy, wz, py, pz)
    return new_phase, new_solute, jnp.transpose(latent.reshape(4, 4, LANES), (0, 2, 1))


def solution(mesh):
    in_specs = (P("gx", "gy", None), P("gx", "gy", None), P("gx", None, "gy"))
    out_specs = (P("gx", "gy", None), P("gx", "gy", None), P("gx", None, "gy"))
    return jax.shard_map(
        functools.partial(body, mesh.shape["gx"], mesh.shape["gy"]),
        mesh=mesh, in_specs=in_specs, out_specs=out_specs, check_vma=False)
```

```python
import functools

import jax
import jax.numpy as jnp
import numpy as np
from jax import lax
from jax.experimental import pallas as pl
from jax.experimental.pallas import tpu as pltpu
from jax.sharding import PartitionSpec as P

MESH = pl.DeviceIdType.MESH

BX, BY = 16, 32
M = 4
EX = BX + 2 * M
RY = 8
EY = 48
LANES = 128
ROOT = 0.025 ** 0.5
ROWS = (4, 12, 20, 28, 36)
OWN = (8, 16, 24, 32)


def tables():
    wy = np.zeros((128, 4 * LANES), np.float32)
    for row in range(40):
        y = row - 4
        low = (2 * y - 3) // 8
        frac = (2 * y - 3 - 8 * low) / 8.0
        for hit, weight in ((low + 1, 1.0 - frac), (low + 2, frac)):
            if 0 <= hit < 10:
                for z in range(4):
                    wy[32 * z + hit, LANES * z + row] += weight
    wz = np.zeros((64, 256), np.float32)
    for fine in range(256):
        low = (2 * fine - 3) // 8
        frac = (2 * fine - 3 - 8 * low) / 8.0
        for hit, weight in ((low, 1.0 - frac), (low + 1, frac)):
            hit = min(max(hit, 0), 63)
            wz[16 * (hit % 4) + hit // 4, fine] += weight
    py = np.zeros((32, 128), np.float32)
    for row in range(128):
        py[row // 4, row] = 1.0
    pz = np.zeros((64, 256), np.float32)
    for fine in range(256):
        z = fine // 4
        pz[16 * (z % 4) + z // 4, fine] = 1.0 / 128.0
    tall = [np.concatenate([t] * 3, axis=0) for t in (wy, wz)]
    wide = [np.concatenate([t] * 3, axis=1) for t in (py, pz)]
    return [jnp.asarray(t, jnp.bfloat16) for t in tall + wide]


def three(value, axis):
    high = value.astype(jnp.bfloat16)
    rest = value - high.astype(jnp.float32)
    middle = rest.astype(jnp.bfloat16)
    low = (rest - middle.astype(jnp.float32)).astype(jnp.bfloat16)
    return jnp.concatenate([high, middle, low], axis=axis)


def kernel(nx, ny, p_in, c_in, m_in, wy_in, wz_in, py_in, pz_in, out, lat_v,
           pc0, pc1, fx, fy, fz, th, lat, wy, wz, py, pz, mac, s1, r1, xs, xr, s2, r2,
           load_sem, x_send, x_recv, y_send, y_recv, d_send, d_recv, t_send, t_recv, h_send, h_recv, l_send, l_recv):
    a = lax.axis_index("gx")
    b = lax.axis_index("gy")
    up_x, down_x = lax.rem(a + 1, nx), lax.rem(a + nx - 1, nx)
    up_y, down_y = lax.rem(b + 1, ny), lax.rem(b + ny - 1, ny)

    loads = []
    for f, src in enumerate((p_in, c_in)):
        for h in range(2):
            loads.append(pltpu.make_async_copy(
                src.at[:, :, pl.ds(h * LANES, LANES)],
                pc0.at[f, h, pl.ds(M, BX), pl.ds(RY, BY), :],
                load_sem.at[2 * f + h]))
    for k, (src, dst) in enumerate(((m_in, mac), (wy_in, wy), (wz_in, wz), (py_in, py), (pz_in, pz))):
        loads.append(pltpu.make_async_copy(src, dst, load_sem.at[4 + k]))
    loads[4].start()
    for copy in loads[:4] + loads[5:]:
        copy.start()

    barrier = pltpu.get_barrier_semaphore()
    corners = ((up_x, up_y), (up_x, down_y), (down_x, up_y), (down_x, down_y))
    peers = [(up_x, b), (down_x, b)] + list(corners)
    for k in range(1, ny):
        peers.append((a, lax.rem(b + k, ny)))
    for peer in peers:
        pl.semaphore_signal(barrier, inc=1, device_id=peer, device_id_type=MESH)

    lane = lax.broadcasted_iota(jnp.int32, (8, LANES), 1)
    first, last = lane == 0, lane == LANES - 1
    first2, last2 = lane < 2, lane >= LANES - 2

    loads[4].wait()
    lane4 = lax.broadcasted_iota(jnp.int32, (4, LANES), 1)
    zone = lane4 // 32
    layers = [mac[pl.ds(z, 4, stride=4), :] for z in range(4)]
    for dest in range(16):
        parts = [pltpu.roll(layers[z], (32 * z - 8 * dest + 1) % LANES, 1) for z in range(4)]
        tile = jnp.where(zone == 0, parts[0], jnp.where(zone == 1, parts[1], jnp.where(zone == 2, parts[2], parts[3])))
        s1[pl.ds(8 * dest, 4), :] = tile

    for copy in loads[:4]:
        copy.wait()
    pl.semaphore_wait(barrier, len(peers))

    x_copies, y_copies, d_copies = [], [], []
    lo, hi = pl.ds(M, M), pl.ds(BX, M)
    before, after = pl.ds(0, M), pl.ds(M + BX, M)
    row_lo, row_hi = pl.ds(RY, M), pl.ds(RY + BY - M, M)
    row_before, row_after = pl.ds(RY - M, M), pl.ds(RY + BY, M)
    rows, planes = pl.ds(RY, BY), pl.ds(M, BX)

    def remote(src, dst, send, recv, peer):
        return pltpu.make_async_remote_copy(
            src_ref=src, dst_ref=dst, send_sem=send, recv_sem=recv, device_id=peer, device_id_type=MESH)

    for k, (src, dst, peer) in enumerate(((hi, before, (up_x, b)), (lo, after, (down_x, b)))):
        x_copies.append(remote(pc0.at[:, :, src, rows, :], pc0.at[:, :, dst, rows, :], x_send.at[k], x_recv.at[k], peer))
    for k, (src, dst, peer) in enumerate(((row_hi, row_before, (a, up_y)), (row_lo, row_after, (a, down_y)))):
        y_copies.append(remote(pc0.at[:, :, planes, src, :], pc0.at[:, :, planes, dst, :], y_send.at[k], y_recv.at[k], peer))
    for k, (sx, dx, sy, dy, peer) in enumerate((
        (hi, before, row_hi, row_before, corners[0]),
        (hi, before, row_lo, row_after, corners[1]),
        (lo, after, row_hi, row_before, corners[2]),
        (lo, after, row_lo, row_after, corners[3]),
    )):
        d_copies.append(remote(pc0.at[:, :, sx, sy, :], pc0.at[:, :, dx, dy, :], d_send.at[k], d_recv.at[k], peer))

    def exchange(src, dst, send, recv):
        far, near, core = b // 8, (b // 2) % 4, b % 2
        steps = [(df, dn, dc) for df in (1, 0) for dn in (2, 1, 3, 0) for dc in (0, 1)]
        steps.sort(key=lambda d: -(2 * d[0] + min(d[1], 4 - d[1])))
        out = []
        for k, (df, dn, dc) in enumerate(d for d in steps if any(d)):
            to = ((far + df) % 2) * 8 + ((near + dn) % 4) * 2 + (core + dc) % 2
            out.append(remote(
                src.at[pl.ds(pl.multiple_of(8 * to, 8), 8), :], dst.at[pl.ds(pl.multiple_of(8 * b, 8), 8), :],
                send.at[k], recv.at[k], (a, to)))
        return out

    here = pl.ds(pl.multiple_of(8 * b, 8), 8)
    t_copies = exchange(s1, r1, t_send, t_recv)
    for copy in t_copies + x_copies + y_copies + d_copies:
        copy.start()
    r1[here, :] = s1[here, :]
    for copy in t_copies:
        copy.wait_recv()
    xs[0] = r1[pl.ds(3, 16, stride=8), :]
    xs[1] = r1[pl.ds(0, 16, stride=8), :]
    h_copies = [remote(xs.at[0], xr.at[0], h_send.at[0], h_recv.at[0], (up_x, b)),
                remote(xs.at[1], xr.at[1], h_send.at[1], h_recv.at[1], (down_x, b))]
    for copy in h_copies:
        copy.start()

    def flux(p, e):
        for r in ROWS:
            at = pl.ds(r, 8)
            v = [p[0, h, e, at, :] for h in range(2)]
            fwd = [pltpu.roll(v[h], 1, 1) for h in range(2)]
            bwd = [pltpu.roll(v[h], LANES - 1, 1) for h in range(2)]
            gz = [jnp.where(last, bwd[1], bwd[0]) - jnp.where(first, v[0], fwd[0]),
                  jnp.where(last, v[1], bwd[1]) - jnp.where(first, fwd[0], fwd[1])]
            wz_ = []
            for h in range(2):
                gx = p[0, h, e + 1, at, :] - p[0, h, e - 1, at, :]
                gy = p[0, h, e, pl.ds(r + 1, 8), :] - p[0, h, e, pl.ds(r - 1, 8), :]
                sx, sy = gx * gx, gy * gy
                total = sx + sy
                planar = total + 4.0
                ratio = (total * total - 8.0 * (sx * sy)) / (planar * planar)
                factor = ROOT + (0.3 * ROOT) * ratio
                stiff = factor * factor
                fx[h, e, at, :] = stiff * gx
                fy[h, e, at, :] = stiff * gy
                wz_.append(stiff * gz[h])
            fwd = [pltpu.roll(w, 1, 1) for w in wz_]
            bwd = [pltpu.roll(w, LANES - 1, 1) for w in wz_]
            fz[0, e, at, :] = jnp.where(last, bwd[1], bwd[0]) - jnp.where(first, 0.0, fwd[0])
            fz[1, e, at, :] = jnp.where(last, 0.0, bwd[1]) - jnp.where(first, fwd[0], fwd[1])

    def update(p, c, e, r, theta, store):
        at = pl.ds(r, 8)
        v = [c[1, h, e, at, :] for h in range(2)]
        fwd = [pltpu.roll(v[h], 2, 1) for h in range(2)]
        bwd = [pltpu.roll(v[h], LANES - 2, 1) for h in range(2)]
        head = jnp.where(first, v[0], pltpu.roll(v[0], 1, 1))
        tail = jnp.where(last, v[1], pltpu.roll(v[1], LANES - 1, 1))
        lz = [jnp.where(last2, bwd[1], bwd[0]) + jnp.where(first2, head, fwd[0]),
              jnp.where(last2, tail, bwd[1]) + jnp.where(first2, fwd[0], fwd[1])]
        for h in range(2):
            div = (fx[h, e + 1, at, :] - fx[h, e - 1, at, :]
                   + (fy[h, e, pl.ds(r + 1, 8), :] - fy[h, e, pl.ds(r - 1, 8), :]) + fz[h, e, at, :])
            old = p[0, h, e, at, :]
            conc = v[h]
            square = 1.0 - old * old
            step = square * (0.1 * old - 0.2 * (square * (theta[h] + conc))) + div
            lap = (c[1, h, e + 2, at, :] + c[1, h, e - 2, at, :]
                   + (c[1, h, e, pl.ds(r + 2, 8), :] + c[1, h, e, pl.ds(r - 2, 8), :]) + lz[h])
            store(h, old + step, 0.85 * conc + (0.025 * lap + 0.5 * step))

    def flux_planes(p, start, gap, count):
        def run(i, carry):
            for q in range(count):
                flux(p, start + gap * i + q)
            return carry
        return run

    def first_update(group):
        e0 = 4 * group + 2
        for r in ROWS:
            at = pl.ds(r, 8)
            low = [th[group, h, at, :] for h in range(2)]
            rise = [th[group + 1, h, at, :] - low[h] for h in range(2)]
            for q in range(4):
                theta = [low[h] + (0.125 + 0.25 * q) * rise[h] for h in range(2)]
                def store(h, new_p, new_c):
                    pc1[0, h, e0 + q, at, :] = new_p
                    pc1[1, h, e0 + q, at, :] = new_c
                update(pc0, pc0, e0 + q, r, theta, store)

    def second_update(group):
        e0 = 4 * group + 4
        for r in OWN:
            at = pl.ds(r, 8)
            to = pl.ds(r - RY, 8)
            total = [None, None]
            for q in range(4):
                low = [th[group + q // 2, h, at, :] for h in range(2)]
                rise = [th[group + q // 2 + 1, h, at, :] - low[h] for h in range(2)]
                frac = 0.125 + 0.25 * ((q + 2) % 4)
                theta = [low[h] + frac * rise[h] for h in range(2)]
                def store(h, new_p, new_c):
                    out[0, h, e0 + q - M, to, :] = new_p
                    out[1, h, e0 + q - M, to, :] = new_c
                    change = new_p - pc0[0, h, e0 + q, at, :]
                    total[h] = change if total[h] is None else total[h] + change
                update(pc1, pc1, e0 + q, r, theta, store)
            for h in range(2):
                lat[pl.ds(pl.multiple_of(BY * group + r - RY, 8), 8), pl.ds(h * LANES, LANES)] = total[h]

    for copy in y_copies:
        copy.wait_recv()
    lax.fori_loop(0, 2, flux_planes(pc0, 5, 7, 7), 0)

    for copy in loads[5:]:
        copy.wait()

    def temperature(first_x, coarse):
        count = len(coarse)
        on_rows = jnp.dot(three(jnp.concatenate(coarse, axis=0), 1), wy[...], preferred_element_type=jnp.float32)
        parts = []
        for x in range(count):
            part = jnp.concatenate([on_rows[16 * x:16 * x + 16, LANES * z:LANES * z + LANES] for z in range(4)], axis=0)
            parts.append(jnp.transpose(part)[:40])
        full = jnp.dot(three(jnp.concatenate(parts, axis=0), 1), wz[...], preferred_element_type=jnp.float32)
        for x in range(count):
            for h in range(2):
                th[first_x[x], h, pl.ds(4, 40), :] = full[40 * x:40 * x + 40, LANES * h:LANES * h + LANES]

    temperature((1, 2, 3, 4), [r1[pl.ds(x, 16, stride=8), :] for x in range(4)])
    lax.fori_loop(1, 4, lambda i, carry: (first_update(i), carry)[1], 0)
    lax.fori_loop(0, 2, flux_planes(pc1, 7, 5, 5), 0)
    lax.fori_loop(1, 3, lambda i, carry: (second_update(i), carry)[1], 0)
    for copy in h_copies:
        copy.wait_recv()
    temperature((0, 5), [xr[0], xr[1]])

    for copy in x_copies + d_copies:
        copy.wait_recv()
    lax.fori_loop(0, 2, flux_planes(pc0, 1, 18, 4), 0)
    lax.fori_loop(0, 2, lambda i, carry: (first_update(4 * i), carry)[1], 0)
    lax.fori_loop(0, 2, flux_planes(pc1, 3, 14, 4), 0)
    lax.fori_loop(0, 2, lambda i, carry: (second_update(3 * i), carry)[1], 0)

    on_y = jnp.dot(py[...], three(lat[...], 0), preferred_element_type=jnp.float32)
    on_z = lax.dot_general(pz[...], three(on_y, 1), (((1,), (1,)), ((), ())), preferred_element_type=jnp.float32)
    for z in range(4):
        s2[pl.ds(z, 16, stride=8), pl.ds(0, 32)] = on_z[16 * z:16 * z + 16]
    l_copies = exchange(s2, r2, l_send, l_recv)
    for copy in l_copies:
        copy.start()
    r2[here, :] = s2[here, :]
    for copy in l_copies:
        copy.wait_recv()
    block = lane4 // 8
    for x in range(4):
        row = None
        for s in range(16):
            part = pltpu.roll(r2[pl.ds(8 * s, 4), :], (8 * s - 8 * x) % LANES, 1)
            row = part if row is None else jnp.where(block == s, part, row)
        lat_v[pl.ds(4 * x, 4), :] = row

    for copy in x_copies + y_copies + d_copies + t_copies + h_copies + l_copies:
        copy.wait_send()


def store_kernel(field, lat, p_out, c_out, lat_out, sem):
    copies = [pltpu.make_async_copy(lat, lat_out, sem.at[4])]
    for f, dst in enumerate((p_out, c_out)):
        for h in range(2):
            copies.append(pltpu.make_async_copy(field.at[f, h], dst.at[:, :, pl.ds(h * LANES, LANES)], sem.at[2 * f + h]))
    for copy in copies:
        copy.start()
    for copy in copies:
        copy.wait()


def body(nx, ny, phase, solute, macro_temp):
    macro = jnp.transpose(macro_temp, (0, 2, 1)).reshape(16, LANES)
    weights = tables()
    f32 = jnp.float32
    anywhere = pl.BlockSpec(memory_space=pl.ANY)
    here = pl.BlockSpec(memory_space=pltpu.VMEM)
    wide = pltpu.VMEM((2, EX, EY, LANES), f32)
    both = pltpu.VMEM((2, 2, EX, EY, LANES), f32)
    dma = pltpu.SemaphoreType.DMA
    field, latent = pl.pallas_call(
        functools.partial(kernel, nx, ny),
        out_shape=(pltpu.VMEM((2, 2, BX, BY, LANES), f32), pltpu.VMEM((16, LANES), f32)),
        in_specs=[anywhere] * 7,
        out_specs=(here, here),
        scratch_shapes=[both] * 2 + [wide] * 3 + [
            pltpu.VMEM((6, 2, EY, LANES), f32),
            pltpu.VMEM((4 * BY, 2 * LANES), f32)] + [
            pltpu.VMEM(w.shape, w.dtype) for w in weights] + [
            pltpu.VMEM((16, LANES), f32),
            pltpu.VMEM((128, LANES), f32), pltpu.VMEM((128, LANES), f32),
            pltpu.VMEM((2, 16, LANES), f32), pltpu.VMEM((2, 16, LANES), f32),
            pltpu.VMEM((128, LANES), f32), pltpu.VMEM((128, LANES), f32),
            dma((9,)), dma((2,)), dma((2,)), dma((2,)), dma((2,)), dma((4,)), dma((4,)),
            dma((16,)), dma((16,)), dma((2,)), dma((2,)), dma((16,)), dma((16,)),
        ],
        compiler_params=pltpu.CompilerParams(collective_id=0, has_side_effects=True, vmem_limit_bytes=60 << 20),
        name="substeps",
    )(phase, solute, macro, *weights)
    new_phase, new_solute, latent = pl.pallas_call(
        store_kernel,
        out_shape=(jax.ShapeDtypeStruct(phase.shape, f32), jax.ShapeDtypeStruct(solute.shape, f32),
                   jax.ShapeDtypeStruct((16, LANES), f32)),
        in_specs=[anywhere] * 2,
        out_specs=(anywhere,) * 3,
        scratch_shapes=[dma((5,))],
        compiler_params=pltpu.CompilerParams(vmem_limit_bytes=1 << 20),
        name="store",
    )(field, latent)
    return new_phase, new_solute, jnp.transpose(latent.reshape(4, 4, LANES), (0, 2, 1))


def solution(mesh):
    in_specs = (P("gx", "gy", None), P("gx", "gy", None), P("gx", None, "gy"))
    out_specs = (P("gx", "gy", None), P("gx", "gy", None), P("gx", None, "gy"))
    return jax.shard_map(
        functools.partial(body, mesh.shape["gx"], mesh.shape["gy"]),
        mesh=mesh, in_specs=in_specs, out_specs=out_specs, check_vma=False)
```

```python
import functools

import jax
import jax.numpy as jnp
import numpy as np
from jax import lax
from jax.experimental import pallas as pl
from jax.experimental.pallas import tpu as pltpu
from jax.sharding import PartitionSpec as P

MESH = pl.DeviceIdType.MESH

BX, BY = 16, 32
M = 4
EX = BX + 2 * M
RY = 8
EY = 48
LANES = 128
ROOT = 0.025 ** 0.5
ROWS = (4, 12, 20, 28, 36)
OWN = (8, 16, 24, 32)


def tables():
    wy = np.zeros((128, 4 * LANES), np.float32)
    for row in range(40):
        y = row - 4
        low = (2 * y - 3) // 8
        frac = (2 * y - 3 - 8 * low) / 8.0
        for hit, weight in ((low + 1, 1.0 - frac), (low + 2, frac)):
            if 0 <= hit < 10:
                for z in range(4):
                    wy[32 * z + hit, LANES * z + row] += weight
    wz = np.zeros((64, 256), np.float32)
    for fine in range(256):
        low = (2 * fine - 3) // 8
        frac = (2 * fine - 3 - 8 * low) / 8.0
        for hit, weight in ((low, 1.0 - frac), (low + 1, frac)):
            hit = min(max(hit, 0), 63)
            wz[16 * (hit % 4) + hit // 4, fine] += weight
    py = np.zeros((32, 128), np.float32)
    for row in range(128):
        py[row // 4, row] = 1.0
    pz = np.zeros((64, 256), np.float32)
    for fine in range(256):
        z = fine // 4
        pz[16 * (z % 4) + z // 4, fine] = 1.0 / 128.0
    tall = [np.concatenate([t] * 3, axis=0) for t in (wy, wz)]
    wide = [np.concatenate([t] * 3, axis=1) for t in (py, pz)]
    return [jnp.asarray(t, jnp.bfloat16) for t in tall + wide]


def three(value, axis):
    high = value.astype(jnp.bfloat16)
    rest = value - high.astype(jnp.float32)
    middle = rest.astype(jnp.bfloat16)
    low = (rest - middle.astype(jnp.float32)).astype(jnp.bfloat16)
    return jnp.concatenate([high, middle, low], axis=axis)


def kernel(nx, ny, p_in, c_in, m_in, wy_in, wz_in, py_in, pz_in, out, lat_v,
           pc0, pc1, fx, fy, fz, th, lat, wy, wz, py, pz, mac, s1, r1, xs, xr, s2, r2,
           load_sem, x_send, x_recv, y_send, y_recv, d_send, d_recv, t_send, t_recv, h_send, h_recv, l_send, l_recv):
    a = lax.axis_index("gx")
    b = lax.axis_index("gy")
    up_x, down_x = lax.rem(a + 1, nx), lax.rem(a + nx - 1, nx)
    up_y, down_y = lax.rem(b + 1, ny), lax.rem(b + ny - 1, ny)

    loads = []
    for f, src in enumerate((p_in, c_in)):
        for h in range(2):
            loads.append(pltpu.make_async_copy(
                src.at[:, :, pl.ds(h * LANES, LANES)],
                pc0.at[f, h, pl.ds(M, BX), pl.ds(RY, BY), :],
                load_sem.at[2 * f + h]))
    for k, (src, dst) in enumerate(((m_in, mac), (wy_in, wy), (wz_in, wz), (py_in, py), (pz_in, pz))):
        loads.append(pltpu.make_async_copy(src, dst, load_sem.at[4 + k]))
    loads[4].start()
    for copy in loads[:4] + loads[5:]:
        copy.start()

    barrier = pltpu.get_barrier_semaphore()
    corners = ((up_x, up_y), (up_x, down_y), (down_x, up_y), (down_x, down_y))
    peers = [(up_x, b), (down_x, b)] + list(corners)
    for k in range(1, ny):
        peers.append((a, lax.rem(b + k, ny)))
    for peer in peers:
        pl.semaphore_signal(barrier, inc=1, device_id=peer, device_id_type=MESH)

    lane = lax.broadcasted_iota(jnp.int32, (8, LANES), 1)
    first, last = lane == 0, lane == LANES - 1
    first2, last2 = lane < 2, lane >= LANES - 2

    loads[4].wait()
    lane4 = lax.broadcasted_iota(jnp.int32, (4, LANES), 1)
    zone = lane4 // 32
    layers = [mac[pl.ds(z, 4, stride=4), :] for z in range(4)]
    for dest in range(16):
        parts = [pltpu.roll(layers[z], (32 * z - 8 * dest + 1) % LANES, 1) for z in range(4)]
        tile = jnp.where(zone == 0, parts[0], jnp.where(zone == 1, parts[1], jnp.where(zone == 2, parts[2], parts[3])))
        s1[pl.ds(8 * dest, 4), :] = tile

    for copy in loads[:4]:
        copy.wait()
    pl.semaphore_wait(barrier, len(peers))

    x_copies, y_copies, d_copies = [], [], []
    lo, hi = pl.ds(M, M), pl.ds(BX, M)
    before, after = pl.ds(0, M), pl.ds(M + BX, M)
    row_lo, row_hi = pl.ds(RY, M), pl.ds(RY + BY - M, M)
    row_before, row_after = pl.ds(RY - M, M), pl.ds(RY + BY, M)
    rows, planes = pl.ds(RY, BY), pl.ds(M, BX)

    def remote(src, dst, send, recv, peer):
        return pltpu.make_async_remote_copy(
            src_ref=src, dst_ref=dst, send_sem=send, recv_sem=recv, device_id=peer, device_id_type=MESH)

    for k, (src, dst, peer) in enumerate(((hi, before, (up_x, b)), (lo, after, (down_x, b)))):
        x_copies.append(remote(pc0.at[:, :, src, rows, :], pc0.at[:, :, dst, rows, :], x_send.at[k], x_recv.at[k], peer))
    for k, (src, dst, peer) in enumerate(((row_hi, row_before, (a, up_y)), (row_lo, row_after, (a, down_y)))):
        y_copies.append(remote(pc0.at[:, :, planes, src, :], pc0.at[:, :, planes, dst, :], y_send.at[k], y_recv.at[k], peer))
    first3, last3, before3, after3 = pl.ds(M, 3), pl.ds(BX + 1, 3), pl.ds(1, 3), pl.ds(M + BX, 3)
    rows_lo, rows_hi, rows_before, rows_after = pl.ds(RY, 3), pl.ds(RY + BY - 3, 3), pl.ds(RY - 3, 3), pl.ds(RY + BY, 3)
    for k, (sx, dx, sy, dy, peer) in enumerate((
        (last3, before3, rows_hi, rows_before, corners[0]),
        (last3, before3, rows_lo, rows_after, corners[1]),
        (first3, after3, rows_hi, rows_before, corners[2]),
        (first3, after3, rows_lo, rows_after, corners[3]),
    )):
        d_copies.append(remote(pc0.at[:, :, sx, sy, :], pc0.at[:, :, dx, dy, :], d_send.at[k], d_recv.at[k], peer))

    def exchange(src, dst, send, recv):
        far, near, core = b // 8, (b // 2) % 4, b % 2
        steps = [(df, dn, dc) for df in (1, 0) for dn in (2, 1, 3, 0) for dc in (0, 1)]
        steps.sort(key=lambda d: -(2 * d[0] + min(d[1], 4 - d[1])))
        out = []
        for k, (df, dn, dc) in enumerate(d for d in steps if any(d)):
            to = ((far + df) % 2) * 8 + ((near + dn) % 4) * 2 + (core + dc) % 2
            out.append(remote(
                src.at[pl.ds(pl.multiple_of(8 * to, 8), 8), :], dst.at[pl.ds(pl.multiple_of(8 * b, 8), 8), :],
                send.at[k], recv.at[k], (a, to)))
        return out

    here = pl.ds(pl.multiple_of(8 * b, 8), 8)
    t_copies = exchange(s1, r1, t_send, t_recv)
    for copy in d_copies + t_copies + y_copies + x_copies:
        copy.start()
    r1[here, :] = s1[here, :]
    def flux(p, planes_):
        tiles = [(e, pl.ds(r, 8), r) for e in planes_ for r in ROWS]
        for e, at, r in tiles:
            v = [p[0, h, e, at, :] for h in range(2)]
            fwd = [pltpu.roll(v[h], 1, 1) for h in range(2)]
            bwd = [pltpu.roll(v[h], LANES - 1, 1) for h in range(2)]
            fz[0, e, at, :] = jnp.where(last, bwd[1], bwd[0]) - jnp.where(first, v[0], fwd[0])
            fz[1, e, at, :] = jnp.where(last, v[1], bwd[1]) - jnp.where(first, fwd[0], fwd[1])
        for e, at, r in tiles:
            for h in range(2):
                gx = p[0, h, e + 1, at, :] - p[0, h, e - 1, at, :]
                gy = p[0, h, e, pl.ds(r + 1, 8), :] - p[0, h, e, pl.ds(r - 1, 8), :]
                sx, sy = gx * gx, gy * gy
                total = sx + sy
                planar = total + 4.0
                ratio = (total * total - 8.0 * (sx * sy)) / (planar * planar)
                factor = ROOT + (0.3 * ROOT) * ratio
                stiff = factor * factor
                fx[h, e, at, :] = stiff * gx
                fy[h, e, at, :] = stiff * gy
                fz[h, e, at, :] = stiff * fz[h, e, at, :]
        for e, at, r in tiles:
            w = [fz[h, e, at, :] for h in range(2)]
            fwd = [pltpu.roll(w[h], 1, 1) for h in range(2)]
            bwd = [pltpu.roll(w[h], LANES - 1, 1) for h in range(2)]
            fz[0, e, at, :] = jnp.where(last, bwd[1], bwd[0]) - jnp.where(first, 0.0, fwd[0])
            fz[1, e, at, :] = jnp.where(last, 0.0, bwd[1]) - jnp.where(first, fwd[0], fwd[1])

    def new_phase(pc, h, e, r, theta):
        at = pl.ds(r, 8)
        div = (fx[h, e + 1, at, :] - fx[h, e - 1, at, :]
               + (fy[h, e, pl.ds(r + 1, 8), :] - fy[h, e, pl.ds(r - 1, 8), :]) + fz[h, e, at, :])
        old, conc = pc[0, h, e, at, :], pc[1, h, e, at, :]
        square = 1.0 - old * old
        step = square * (0.1 * old - 0.2 * (square * (theta + conc))) + div
        return old + step, step

    def new_solute(pc, e, r, steps):
        at = pl.ds(r, 8)
        v = [pc[1, h, e, at, :] for h in range(2)]
        fwd = [pltpu.roll(v[h], 2, 1) for h in range(2)]
        bwd = [pltpu.roll(v[h], LANES - 2, 1) for h in range(2)]
        head = jnp.where(first, v[0], pltpu.roll(v[0], 1, 1))
        tail = jnp.where(last, v[1], pltpu.roll(v[1], LANES - 1, 1))
        lz = [jnp.where(last2, bwd[1], bwd[0]) + jnp.where(first2, head, fwd[0]),
              jnp.where(last2, tail, bwd[1]) + jnp.where(first2, fwd[0], fwd[1])]
        out = []
        for h in range(2):
            lap = (pc[1, h, e + 2, at, :] + pc[1, h, e - 2, at, :]
                   + (pc[1, h, e, pl.ds(r + 2, 8), :] + pc[1, h, e, pl.ds(r - 2, 8), :]) + lz[h])
            out.append(0.85 * v[h] + (0.025 * lap + 0.5 * steps[h]))
        return out

    def flux_planes(p, start, gap, count):
        def run(i, carry):
            flux(p, [start + gap * i + q for q in range(count)])
            return carry
        return run

    def first_update(group):
        e0 = 4 * group + 2
        for r in ROWS:
            at = pl.ds(r, 8)
            low = [th[group, h, at, :] for h in range(2)]
            rise = [th[group + 1, h, at, :] - low[h] for h in range(2)]
            for q in range(4):
                steps = []
                for h in range(2):
                    new, step = new_phase(pc0, h, e0 + q, r, low[h] + (0.125 + 0.25 * q) * rise[h])
                    pc1[0, h, e0 + q, at, :] = new
                    steps.append(step)
                for h, new in enumerate(new_solute(pc0, e0 + q, r, steps)):
                    pc1[1, h, e0 + q, at, :] = new

    def second_update(group, with_solute):
        e0 = 4 * group + 4
        for r in OWN:
            at = pl.ds(r, 8)
            to = pl.ds(r - RY, 8)
            total = [None, None]
            for q in range(4):
                frac = 0.125 + 0.25 * ((q + 2) % 4)
                steps = []
                for h in range(2):
                    low = th[group + q // 2, h, at, :]
                    new, step = new_phase(pc1, h, e0 + q, r, low + frac * (th[group + q // 2 + 1, h, at, :] - low))
                    out[0, h, e0 + q - M, to, :] = new
                    change = new - pc0[0, h, e0 + q, at, :]
                    total[h] = change if total[h] is None else total[h] + change
                    steps.append(step)
                if with_solute:
                    for h, new in enumerate(new_solute(pc1, e0 + q, r, steps)):
                        out[1, h, e0 + q - M, to, :] = new
            for h in range(2):
                lat[pl.ds(pl.multiple_of(BY * group + r - RY, 8), 8), pl.ds(h * LANES, LANES)] = total[h]

    def late_solute(group):
        e0 = 4 * group + 4
        for r in OWN:
            to = pl.ds(r - RY, 8)
            for q in range(4):
                steps = [out[0, h, e0 + q - M, to, :] - pc1[0, h, e0 + q, pl.ds(r, 8), :] for h in range(2)]
                for h, new in enumerate(new_solute(pc1, e0 + q, r, steps)):
                    out[1, h, e0 + q - M, to, :] = new

    for copy in y_copies:
        copy.wait_recv()
    lax.fori_loop(0, 2, flux_planes(pc0, 5, 7, 7), 0)
    for copy in t_copies:
        copy.wait_recv()
    xs[0] = r1[pl.ds(3, 16, stride=8), :]
    xs[1] = r1[pl.ds(0, 16, stride=8), :]
    h_copies = [remote(xs.at[0], xr.at[0], h_send.at[0], h_recv.at[0], (up_x, b)),
                remote(xs.at[1], xr.at[1], h_send.at[1], h_recv.at[1], (down_x, b))]
    for copy in h_copies:
        copy.start()


    for copy in loads[5:]:
        copy.wait()

    def temperature(first_x, coarse):
        count = len(coarse)
        on_rows = jnp.dot(three(jnp.concatenate(coarse, axis=0), 1), wy[...], preferred_element_type=jnp.float32)
        parts = []
        for x in range(count):
            part = jnp.concatenate([on_rows[16 * x:16 * x + 16, LANES * z:LANES * z + LANES] for z in range(4)], axis=0)
            parts.append(jnp.transpose(part)[:40])
        full = jnp.dot(three(jnp.concatenate(parts, axis=0), 1), wz[...], preferred_element_type=jnp.float32)
        for x in range(count):
            for h in range(2):
                th[first_x[x], h, pl.ds(4, 40), :] = full[40 * x:40 * x + 40, LANES * h:LANES * h + LANES]

    temperature((1, 2, 3, 4), [r1[pl.ds(x, 16, stride=8), :] for x in range(4)])
    lax.fori_loop(1, 4, lambda i, carry: (first_update(i), carry)[1], 0)
    lax.fori_loop(0, 2, flux_planes(pc1, 7, 5, 5), 0)
    lax.fori_loop(1, 3, lambda i, carry: (second_update(i, True), carry)[1], 0)

    for side in (1, 0):
        for copy in [x_copies[side]] + d_copies[2 * side:2 * side + 2]:
            copy.wait_recv()
        flux(pc0, [(1, 19)[side] + q for q in range(4)])
        h_copies[side].wait_recv()
        temperature(((0,), (5,))[side], [xr[side]])
        first_update((0, 4)[side])
        flux(pc1, [(3, 17)[side] + q for q in range(4)])
        second_update((0, 3)[side], False)

    on_y = jnp.dot(py[...], three(lat[...], 0), preferred_element_type=jnp.float32)
    on_z = lax.dot_general(pz[...], three(on_y, 1), (((1,), (1,)), ((), ())), preferred_element_type=jnp.float32)
    for z in range(4):
        s2[pl.ds(z, 16, stride=8), pl.ds(0, 32)] = on_z[16 * z:16 * z + 16]
    l_copies = exchange(s2, r2, l_send, l_recv)
    for copy in l_copies:
        copy.start()
    r2[here, :] = s2[here, :]
    lax.fori_loop(0, 2, lambda i, carry: (late_solute(3 * i), carry)[1], 0)
    for copy in l_copies:
        copy.wait_recv()
    block = lane4 // 8
    for x in range(4):
        row = None
        for s in range(16):
            part = pltpu.roll(r2[pl.ds(8 * s, 4), :], (8 * s - 8 * x) % LANES, 1)
            row = part if row is None else jnp.where(block == s, part, row)
        lat_v[pl.ds(4 * x, 4), :] = row

    for copy in x_copies + y_copies + d_copies + t_copies + h_copies + l_copies:
        copy.wait_send()


def store_kernel(field, lat, p_out, c_out, lat_out, sem):
    copies = [pltpu.make_async_copy(lat, lat_out, sem.at[4])]
    for f, dst in enumerate((p_out, c_out)):
        for h in range(2):
            copies.append(pltpu.make_async_copy(field.at[f, h], dst.at[:, :, pl.ds(h * LANES, LANES)], sem.at[2 * f + h]))
    for copy in copies:
        copy.start()
    for copy in copies:
        copy.wait()


def body(nx, ny, phase, solute, macro_temp):
    macro = jnp.transpose(macro_temp, (0, 2, 1)).reshape(16, LANES)
    weights = tables()
    f32 = jnp.float32
    anywhere = pl.BlockSpec(memory_space=pl.ANY)
    here = pl.BlockSpec(memory_space=pltpu.VMEM)
    wide = pltpu.VMEM((2, EX, EY, LANES), f32)
    both = pltpu.VMEM((2, 2, EX, EY, LANES), f32)
    dma = pltpu.SemaphoreType.DMA
    field, latent = pl.pallas_call(
        functools.partial(kernel, nx, ny),
        out_shape=(pltpu.VMEM((2, 2, BX, BY, LANES), f32), pltpu.VMEM((16, LANES), f32)),
        in_specs=[anywhere] * 7,
        out_specs=(here, here),
        scratch_shapes=[both] * 2 + [wide] * 3 + [
            pltpu.VMEM((6, 2, EY, LANES), f32),
            pltpu.VMEM((4 * BY, 2 * LANES), f32)] + [
            pltpu.VMEM(w.shape, w.dtype) for w in weights] + [
            pltpu.VMEM((16, LANES), f32),
            pltpu.VMEM((128, LANES), f32), pltpu.VMEM((128, LANES), f32),
            pltpu.VMEM((2, 16, LANES), f32), pltpu.VMEM((2, 16, LANES), f32),
            pltpu.VMEM((128, LANES), f32), pltpu.VMEM((128, LANES), f32),
            dma((9,)), dma((2,)), dma((2,)), dma((2,)), dma((2,)), dma((4,)), dma((4,)),
            dma((16,)), dma((16,)), dma((2,)), dma((2,)), dma((16,)), dma((16,)),
        ],
        compiler_params=pltpu.CompilerParams(collective_id=0, has_side_effects=True, vmem_limit_bytes=60 << 20),
        name="substeps",
    )(phase, solute, macro, *weights)
    new_phase, new_solute, latent = pl.pallas_call(
        store_kernel,
        out_shape=(jax.ShapeDtypeStruct(phase.shape, f32), jax.ShapeDtypeStruct(solute.shape, f32),
                   jax.ShapeDtypeStruct((16, LANES), f32)),
        in_specs=[anywhere] * 2,
        out_specs=(anywhere,) * 3,
        scratch_shapes=[dma((5,))],
        compiler_params=pltpu.CompilerParams(vmem_limit_bytes=1 << 20),
        name="store",
    )(field, latent)
    return new_phase, new_solute, jnp.transpose(latent.reshape(4, 4, LANES), (0, 2, 1))


def solution(mesh):
    in_specs = (P("gx", "gy", None), P("gx", "gy", None), P("gx", None, "gy"))
    out_specs = (P("gx", "gy", None), P("gx", "gy", None), P("gx", None, "gy"))
    return jax.shard_map(
        functools.partial(body, mesh.shape["gx"], mesh.shape["gy"]),
        mesh=mesh, in_specs=in_specs, out_specs=out_specs, check_vma=False)
```

```python
import functools

import jax
import jax.numpy as jnp
import numpy as np
from jax import lax
from jax.experimental import pallas as pl
from jax.experimental.pallas import tpu as pltpu
from jax.sharding import PartitionSpec as P

MESH = pl.DeviceIdType.MESH

BX, BY = 16, 32
M = 4
EX = BX + 2 * M
RY = 8
EY = 48
LANES = 128
ROOT = 0.025 ** 0.5
ROWS = (4, 12, 20, 28, 36)
OWN = (8, 16, 24, 32)


def tables():
    wy = np.zeros((128, 4 * LANES), np.float32)
    for row in range(40):
        y = row - 4
        low = (2 * y - 3) // 8
        frac = (2 * y - 3 - 8 * low) / 8.0
        for hit, weight in ((low + 1, 1.0 - frac), (low + 2, frac)):
            if 0 <= hit < 10:
                for z in range(4):
                    wy[32 * z + hit, LANES * z + row] += weight
    wz = np.zeros((64, 256), np.float32)
    for fine in range(256):
        low = (2 * fine - 3) // 8
        frac = (2 * fine - 3 - 8 * low) / 8.0
        for hit, weight in ((low, 1.0 - frac), (low + 1, frac)):
            hit = min(max(hit, 0), 63)
            wz[16 * (hit % 4) + hit // 4, fine] += weight
    py = np.zeros((32, 128), np.float32)
    for row in range(128):
        py[row // 4, row] = 1.0
    pz = np.zeros((64, 256), np.float32)
    for fine in range(256):
        z = fine // 4
        pz[16 * (z % 4) + z // 4, fine] = 1.0 / 128.0
    tall = [np.concatenate([t] * 3, axis=0) for t in (wy, wz)]
    wide = [np.concatenate([t] * 3, axis=1) for t in (py, pz)]
    return [jnp.asarray(t, jnp.bfloat16) for t in tall + wide]


def three(value, axis):
    high = value.astype(jnp.bfloat16)
    rest = value - high.astype(jnp.float32)
    middle = rest.astype(jnp.bfloat16)
    low = (rest - middle.astype(jnp.float32)).astype(jnp.bfloat16)
    return jnp.concatenate([high, middle, low], axis=axis)


def kernel(nx, ny, p_in, c_in, m_in, wy_in, wz_in, py_in, pz_in, out, lat_v,
           pc0, pc1, fx, fy, fz, th, lat, wy, wz, py, pz, mac, s1, r1, xs, xr, s2, r2,
           load_sem, x_send, x_recv, y_send, y_recv, d_send, d_recv, t_send, t_recv, h_send, h_recv, l_send, l_recv):
    a = lax.axis_index("gx")
    b = lax.axis_index("gy")
    up_x, down_x = lax.rem(a + 1, nx), lax.rem(a + nx - 1, nx)
    up_y, down_y = lax.rem(b + 1, ny), lax.rem(b + ny - 1, ny)

    loads = []
    for f, src in enumerate((p_in, c_in)):
        for h in range(2):
            loads.append(pltpu.make_async_copy(
                src.at[:, :, pl.ds(h * LANES, LANES)],
                pc0.at[f, h, pl.ds(M, BX), pl.ds(RY, BY), :],
                load_sem.at[2 * f + h]))
    for k, (src, dst) in enumerate(((m_in, mac), (wy_in, wy), (wz_in, wz), (py_in, py), (pz_in, pz))):
        loads.append(pltpu.make_async_copy(src, dst, load_sem.at[4 + k]))
    loads[4].start()
    for copy in loads[:4] + loads[5:]:
        copy.start()

    barrier = pltpu.get_barrier_semaphore()
    corners = ((up_x, up_y), (up_x, down_y), (down_x, up_y), (down_x, down_y))
    peers = [(up_x, b), (down_x, b)] + list(corners)
    for k in range(1, ny):
        peers.append((a, lax.rem(b + k, ny)))
    for peer in peers:
        pl.semaphore_signal(barrier, inc=1, device_id=peer, device_id_type=MESH)

    lane = lax.broadcasted_iota(jnp.int32, (8, LANES), 1)
    first, last = lane == 0, lane == LANES - 1
    first2, last2 = lane < 2, lane >= LANES - 2

    loads[4].wait()
    lane4 = lax.broadcasted_iota(jnp.int32, (4, LANES), 1)
    zone = lane4 // 32
    layers = [mac[pl.ds(z, 4, stride=4), :] for z in range(4)]
    for dest in range(16):
        parts = [pltpu.roll(layers[z], (32 * z - 8 * dest + 1) % LANES, 1) for z in range(4)]
        tile = jnp.where(zone == 0, parts[0], jnp.where(zone == 1, parts[1], jnp.where(zone == 2, parts[2], parts[3])))
        s1[pl.ds(8 * dest, 4), :] = tile

    for copy in loads[:4]:
        copy.wait()
    pl.semaphore_wait(barrier, len(peers))

    x_copies, y_copies, d_copies = [], [], []
    lo, hi = pl.ds(M, M), pl.ds(BX, M)
    before, after = pl.ds(0, M), pl.ds(M + BX, M)
    row_lo, row_hi = pl.ds(RY, M), pl.ds(RY + BY - M, M)
    row_before, row_after = pl.ds(RY - M, M), pl.ds(RY + BY, M)
    rows, planes = pl.ds(RY, BY), pl.ds(M, BX)

    def remote(src, dst, send, recv, peer):
        return pltpu.make_async_remote_copy(
            src_ref=src, dst_ref=dst, send_sem=send, recv_sem=recv, device_id=peer, device_id_type=MESH)

    for k, (src, dst, peer) in enumerate(((hi, before, (up_x, b)), (lo, after, (down_x, b)))):
        x_copies.append(remote(pc0.at[:, :, src, rows, :], pc0.at[:, :, dst, rows, :], x_send.at[k], x_recv.at[k], peer))
    for k, (src, dst, peer) in enumerate(((row_hi, row_before, (a, up_y)), (row_lo, row_after, (a, down_y)))):
        y_copies.append(remote(pc0.at[:, :, planes, src, :], pc0.at[:, :, planes, dst, :], y_send.at[k], y_recv.at[k], peer))
    first3, last3, before3, after3 = pl.ds(M, 3), pl.ds(BX + 1, 3), pl.ds(1, 3), pl.ds(M + BX, 3)
    rows_lo, rows_hi, rows_before, rows_after = pl.ds(RY, 3), pl.ds(RY + BY - 3, 3), pl.ds(RY - 3, 3), pl.ds(RY + BY, 3)
    for k, (sx, dx, sy, dy, peer) in enumerate((
        (last3, before3, rows_hi, rows_before, corners[0]),
        (last3, before3, rows_lo, rows_after, corners[1]),
        (first3, after3, rows_hi, rows_before, corners[2]),
        (first3, after3, rows_lo, rows_after, corners[3]),
    )):
        d_copies.append(remote(pc0.at[:, :, sx, sy, :], pc0.at[:, :, dx, dy, :], d_send.at[k], d_recv.at[k], peer))

    def exchange(src, dst, send, recv):
        far, near, core = b // 8, (b // 2) % 4, b % 2
        steps = [(df, dn, dc) for df in (1, 0) for dn in (2, 1, 3, 0) for dc in (0, 1)]
        steps.sort(key=lambda d: -(2 * d[0] + min(d[1], 4 - d[1])))
        out = []
        for k, (df, dn, dc) in enumerate(d for d in steps if any(d)):
            to = ((far + df) % 2) * 8 + ((near + dn) % 4) * 2 + (core + dc) % 2
            out.append(remote(
                src.at[pl.ds(pl.multiple_of(8 * to, 8), 4), :], dst.at[pl.ds(pl.multiple_of(8 * b, 8), 4), :],
                send.at[k], recv.at[k], (a, to)))
        return out

    here = pl.ds(pl.multiple_of(8 * b, 8), 4)
    t_copies = exchange(s1, r1, t_send, t_recv)
    for copy in t_copies + d_copies + x_copies + y_copies:
        copy.start()
    r1[here, :] = s1[here, :]
    def flux(p, planes_):
        tiles = [(e, pl.ds(r, 8), r) for e in planes_ for r in ROWS]
        for e, at, r in tiles:
            v = [p[0, h, e, at, :] for h in range(2)]
            fwd = [pltpu.roll(v[h], 1, 1) for h in range(2)]
            bwd = [pltpu.roll(v[h], LANES - 1, 1) for h in range(2)]
            fz[0, e, at, :] = jnp.where(last, bwd[1], bwd[0]) - jnp.where(first, v[0], fwd[0])
            fz[1, e, at, :] = jnp.where(last, v[1], bwd[1]) - jnp.where(first, fwd[0], fwd[1])
        for e, at, r in tiles:
            for h in range(2):
                gx = p[0, h, e + 1, at, :] - p[0, h, e - 1, at, :]
                gy = p[0, h, e, pl.ds(r + 1, 8), :] - p[0, h, e, pl.ds(r - 1, 8), :]
                sx, sy = gx * gx, gy * gy
                total = sx + sy
                planar = total + 4.0
                ratio = (total * total - 8.0 * (sx * sy)) / (planar * planar)
                factor = ROOT + (0.3 * ROOT) * ratio
                stiff = factor * factor
                fx[h, e, at, :] = stiff * gx
                fy[h, e, at, :] = stiff * gy
                fz[h, e, at, :] = stiff * fz[h, e, at, :]
        for e, at, r in tiles:
            w = [fz[h, e, at, :] for h in range(2)]
            fwd = [pltpu.roll(w[h], 1, 1) for h in range(2)]
            bwd = [pltpu.roll(w[h], LANES - 1, 1) for h in range(2)]
            fz[0, e, at, :] = jnp.where(last, bwd[1], bwd[0]) - jnp.where(first, 0.0, fwd[0])
            fz[1, e, at, :] = jnp.where(last, 0.0, bwd[1]) - jnp.where(first, fwd[0], fwd[1])

    def new_phase(pc, h, e, r, theta):
        at = pl.ds(r, 8)
        div = (fx[h, e + 1, at, :] - fx[h, e - 1, at, :]
               + (fy[h, e, pl.ds(r + 1, 8), :] - fy[h, e, pl.ds(r - 1, 8), :]) + fz[h, e, at, :])
        old, conc = pc[0, h, e, at, :], pc[1, h, e, at, :]
        square = 1.0 - old * old
        step = square * (0.1 * old - 0.2 * (square * (theta + conc))) + div
        return old + step, step

    def new_solute(pc, e, r, steps):
        at = pl.ds(r, 8)
        v = [pc[1, h, e, at, :] for h in range(2)]
        fwd = [pltpu.roll(v[h], 2, 1) for h in range(2)]
        bwd = [pltpu.roll(v[h], LANES - 2, 1) for h in range(2)]
        head = jnp.where(first, v[0], pltpu.roll(v[0], 1, 1))
        tail = jnp.where(last, v[1], pltpu.roll(v[1], LANES - 1, 1))
        lz = [jnp.where(last2, bwd[1], bwd[0]) + jnp.where(first2, head, fwd[0]),
              jnp.where(last2, tail, bwd[1]) + jnp.where(first2, fwd[0], fwd[1])]
        out = []
        for h in range(2):
            lap = (pc[1, h, e + 2, at, :] + pc[1, h, e - 2, at, :]
                   + (pc[1, h, e, pl.ds(r + 2, 8), :] + pc[1, h, e, pl.ds(r - 2, 8), :]) + lz[h])
            out.append(0.85 * v[h] + (0.025 * lap + 0.5 * steps[h]))
        return out

    def flux_planes(p, start, gap, count):
        def run(i, carry):
            flux(p, [start + gap * i + q for q in range(count)])
            return carry
        return run

    def first_update(group):
        e0 = 4 * group + 2
        for r in ROWS:
            at = pl.ds(r, 8)
            low = [th[group, h, at, :] for h in range(2)]
            rise = [th[group + 1, h, at, :] - low[h] for h in range(2)]
            for q in range(4):
                steps = []
                for h in range(2):
                    new, step = new_phase(pc0, h, e0 + q, r, low[h] + (0.125 + 0.25 * q) * rise[h])
                    pc1[0, h, e0 + q, at, :] = new
                    steps.append(step)
                for h, new in enumerate(new_solute(pc0, e0 + q, r, steps)):
                    pc1[1, h, e0 + q, at, :] = new

    def second_update(group, with_solute):
        e0 = 4 * group + 4
        for r in OWN:
            at = pl.ds(r, 8)
            to = pl.ds(r - RY, 8)
            total = [None, None]
            for q in range(4):
                frac = 0.125 + 0.25 * ((q + 2) % 4)
                steps = []
                for h in range(2):
                    low = th[group + q // 2, h, at, :]
                    new, step = new_phase(pc1, h, e0 + q, r, low + frac * (th[group + q // 2 + 1, h, at, :] - low))
                    out[0, h, e0 + q - M, to, :] = new
                    change = new - pc0[0, h, e0 + q, at, :]
                    total[h] = change if total[h] is None else total[h] + change
                    steps.append(step)
                if with_solute:
                    for h, new in enumerate(new_solute(pc1, e0 + q, r, steps)):
                        out[1, h, e0 + q - M, to, :] = new
            for h in range(2):
                lat[pl.ds(pl.multiple_of(BY * group + r - RY, 8), 8), pl.ds(h * LANES, LANES)] = total[h]

    def late_solute(group):
        e0 = 4 * group + 4
        for r in OWN:
            to = pl.ds(r - RY, 8)
            for q in range(4):
                steps = [out[0, h, e0 + q - M, to, :] - pc1[0, h, e0 + q, pl.ds(r, 8), :] for h in range(2)]
                for h, new in enumerate(new_solute(pc1, e0 + q, r, steps)):
                    out[1, h, e0 + q - M, to, :] = new

    for copy in y_copies:
        copy.wait_recv()
    lax.fori_loop(0, 2, flux_planes(pc0, 5, 7, 7), 0)
    for copy in t_copies:
        copy.wait_recv()
    xs[0] = r1[pl.ds(3, 16, stride=8), :]
    xs[1] = r1[pl.ds(0, 16, stride=8), :]
    h_copies = [remote(xs.at[0], xr.at[0], h_send.at[0], h_recv.at[0], (up_x, b)),
                remote(xs.at[1], xr.at[1], h_send.at[1], h_recv.at[1], (down_x, b))]
    for copy in h_copies:
        copy.start()


    for copy in loads[5:]:
        copy.wait()

    def temperature(first_x, coarse):
        count = len(coarse)
        on_rows = jnp.dot(three(jnp.concatenate(coarse, axis=0), 1), wy[...], preferred_element_type=jnp.float32)
        parts = []
        for x in range(count):
            part = jnp.concatenate([on_rows[16 * x:16 * x + 16, LANES * z:LANES * z + LANES] for z in range(4)], axis=0)
            parts.append(jnp.transpose(part)[:40])
        full = jnp.dot(three(jnp.concatenate(parts, axis=0), 1), wz[...], preferred_element_type=jnp.float32)
        for x in range(count):
            for h in range(2):
                th[first_x[x], h, pl.ds(4, 40), :] = full[40 * x:40 * x + 40, LANES * h:LANES * h + LANES]

    temperature((1, 2, 3, 4), [r1[pl.ds(x, 16, stride=8), :] for x in range(4)])
    lax.fori_loop(1, 4, lambda i, carry: (first_update(i), carry)[1], 0)
    lax.fori_loop(0, 2, flux_planes(pc1, 7, 5, 5), 0)
    lax.fori_loop(1, 3, lambda i, carry: (second_update(i, True), carry)[1], 0)

    for side in (1, 0):
        for copy in [x_copies[side]] + d_copies[2 * side:2 * side + 2]:
            copy.wait_recv()
        flux(pc0, [(1, 19)[side] + q for q in range(4)])
        h_copies[side].wait_recv()
        temperature(((0,), (5,))[side], [xr[side]])
        first_update((0, 4)[side])
        flux(pc1, [(3, 17)[side] + q for q in range(4)])
        second_update((0, 3)[side], False)

    on_y = jnp.dot(py[...], three(lat[...], 0), preferred_element_type=jnp.float32)
    on_z = lax.dot_general(pz[...], three(on_y, 1), (((1,), (1,)), ((), ())), preferred_element_type=jnp.float32)
    for z in range(4):
        s2[pl.ds(z, 16, stride=8), pl.ds(0, 32)] = on_z[16 * z:16 * z + 16]
    l_copies = exchange(s2, r2, l_send, l_recv)
    for copy in l_copies:
        copy.start()
    r2[here, :] = s2[here, :]
    lax.fori_loop(0, 2, lambda i, carry: (late_solute(3 * i), carry)[1], 0)
    for copy in l_copies:
        copy.wait_recv()
    block = lane4 // 8
    for x in range(4):
        row = None
        for s in range(16):
            part = pltpu.roll(r2[pl.ds(8 * s, 4), :], (8 * s - 8 * x) % LANES, 1)
            row = part if row is None else jnp.where(block == s, part, row)
        lat_v[pl.ds(4 * x, 4), :] = row

    for copy in x_copies + y_copies + d_copies + t_copies + h_copies + l_copies:
        copy.wait_send()


def store_kernel(field, lat, p_out, c_out, lat_out, sem):
    copies = [pltpu.make_async_copy(lat, lat_out, sem.at[4])]
    for f, dst in enumerate((p_out, c_out)):
        for h in range(2):
            copies.append(pltpu.make_async_copy(field.at[f, h], dst.at[:, :, pl.ds(h * LANES, LANES)], sem.at[2 * f + h]))
    for copy in copies:
        copy.start()
    for copy in copies:
        copy.wait()


def body(nx, ny, phase, solute, macro_temp):
    macro = jnp.transpose(macro_temp, (0, 2, 1)).reshape(16, LANES)
    weights = tables()
    f32 = jnp.float32
    anywhere = pl.BlockSpec(memory_space=pl.ANY)
    here = pl.BlockSpec(memory_space=pltpu.VMEM)
    wide = pltpu.VMEM((2, EX, EY, LANES), f32)
    both = pltpu.VMEM((2, 2, EX, EY, LANES), f32)
    dma = pltpu.SemaphoreType.DMA
    field, latent = pl.pallas_call(
        functools.partial(kernel, nx, ny),
        out_shape=(pltpu.VMEM((2, 2, BX, BY, LANES), f32), pltpu.VMEM((16, LANES), f32)),
        in_specs=[anywhere] * 7,
        out_specs=(here, here),
        scratch_shapes=[both] * 2 + [wide] * 3 + [
            pltpu.VMEM((6, 2, EY, LANES), f32),
            pltpu.VMEM((4 * BY, 2 * LANES), f32)] + [
            pltpu.VMEM(w.shape, w.dtype) for w in weights] + [
            pltpu.VMEM((16, LANES), f32),
            pltpu.VMEM((128, LANES), f32), pltpu.VMEM((128, LANES), f32),
            pltpu.VMEM((2, 16, LANES), f32), pltpu.VMEM((2, 16, LANES), f32),
            pltpu.VMEM((128, LANES), f32), pltpu.VMEM((128, LANES), f32),
            dma((9,)), dma((2,)), dma((2,)), dma((2,)), dma((2,)), dma((4,)), dma((4,)),
            dma((16,)), dma((16,)), dma((2,)), dma((2,)), dma((16,)), dma((16,)),
        ],
        compiler_params=pltpu.CompilerParams(collective_id=0, has_side_effects=True, vmem_limit_bytes=60 << 20),
        name="substeps",
    )(phase, solute, macro, *weights)
    new_phase, new_solute, latent = pl.pallas_call(
        store_kernel,
        out_shape=(jax.ShapeDtypeStruct(phase.shape, f32), jax.ShapeDtypeStruct(solute.shape, f32),
                   jax.ShapeDtypeStruct((16, LANES), f32)),
        in_specs=[anywhere] * 2,
        out_specs=(anywhere,) * 3,
        scratch_shapes=[dma((5,))],
        compiler_params=pltpu.CompilerParams(vmem_limit_bytes=1 << 20),
        name="store",
    )(field, latent)
    return new_phase, new_solute, jnp.transpose(latent.reshape(4, 4, LANES), (0, 2, 1))


def solution(mesh):
    in_specs = (P("gx", "gy", None), P("gx", "gy", None), P("gx", None, "gy"))
    out_specs = (P("gx", "gy", None), P("gx", "gy", None), P("gx", None, "gy"))
    return jax.shard_map(
        functools.partial(body, mesh.shape["gx"], mesh.shape["gy"]),
        mesh=mesh, in_specs=in_specs, out_specs=out_specs, check_vma=False)
```

```python
import functools

import jax
import jax.numpy as jnp
import numpy as np
from jax import lax
from jax.experimental import pallas as pl
from jax.experimental.pallas import tpu as pltpu
from jax.sharding import PartitionSpec as P

MESH = pl.DeviceIdType.MESH

BX, BY = 16, 32
M = 4
EX = BX + 2 * M
RY = 8
EY = 48
LANES = 128
ROOT = 0.025 ** 0.5
ROWS = (4, 12, 20, 28, 36)
OWN = (8, 16, 24, 32)


def tables():
    wy = np.zeros((128, 4 * LANES), np.float32)
    for row in range(40):
        y = row - 4
        low = (2 * y - 3) // 8
        frac = (2 * y - 3 - 8 * low) / 8.0
        for hit, weight in ((low + 1, 1.0 - frac), (low + 2, frac)):
            if 0 <= hit < 10:
                for z in range(4):
                    wy[32 * z + hit, LANES * z + row] += weight
    wz = np.zeros((64, 256), np.float32)
    for fine in range(256):
        low = (2 * fine - 3) // 8
        frac = (2 * fine - 3 - 8 * low) / 8.0
        for hit, weight in ((low, 1.0 - frac), (low + 1, frac)):
            hit = min(max(hit, 0), 63)
            wz[16 * (hit % 4) + hit // 4, fine] += weight
    py = np.zeros((16, BY), np.float32)
    for row in range(BY):
        py[row // 4, row] = 1.0
    pz = np.zeros((64, 256), np.float32)
    for fine in range(256):
        z = fine // 4
        pz[16 * (z % 4) + z // 4, fine] = 1.0 / 128.0
    tall = [np.concatenate([t] * 3, axis=0) for t in (wy, wz)]
    wide = [np.concatenate([t] * 3, axis=1) for t in (py, pz)]
    return [jnp.asarray(t, jnp.bfloat16) for t in tall + wide]


def three(value, axis):
    high = value.astype(jnp.bfloat16)
    rest = value - high.astype(jnp.float32)
    middle = rest.astype(jnp.bfloat16)
    low = (rest - middle.astype(jnp.float32)).astype(jnp.bfloat16)
    return jnp.concatenate([high, middle, low], axis=axis)


def kernel(nx, ny, p_in, c_in, m_in, wy_in, wz_in, py_in, pz_in, out, lat_v,
           pc0, pc1, fx, fy, fz, th, lat, oy, wy, wz, py, pz, mac, s1, r1, xs, xr, s2, r2,
           load_sem, x_send, x_recv, y_send, y_recv, d_send, d_recv, t_send, t_recv, h_send, h_recv, l_send, l_recv):
    a = lax.axis_index("gx")
    b = lax.axis_index("gy")
    up_x, down_x = lax.rem(a + 1, nx), lax.rem(a + nx - 1, nx)
    up_y, down_y = lax.rem(b + 1, ny), lax.rem(b + ny - 1, ny)

    barrier = pltpu.get_barrier_semaphore()
    corners = ((up_x, up_y), (up_x, down_y), (down_x, up_y), (down_x, down_y))
    far, near, core = b // 8, (b // 2) % 4, b % 2
    steps = [(df, dn, dc) for df in (1, 0) for dn in (2, 1, 3, 0) for dc in (0, 1)][:-2] + [(0, 0, 1)]
    steps.sort(key=lambda d: -(2 * d[0] + min(d[1], 4 - d[1])))
    others = [((far + df) % 2) * 8 + ((near + dn) % 4) * 2 + (core + dc) % 2 for df, dn, dc in steps]
    peers = [(a, to) for to in others[:12]] + list(corners) + [(up_x, b), (down_x, b)] + [(a, to) for to in others[12:]]
    for peer in peers:
        pl.semaphore_signal(barrier, inc=1, device_id=peer, device_id_type=MESH)

    loads = []
    for f, src in enumerate((p_in, c_in)):
        for h in range(2):
            loads.append(pltpu.make_async_copy(
                src.at[:, :, pl.ds(h * LANES, LANES)],
                pc0.at[f, h, pl.ds(M, BX), pl.ds(RY, BY), :],
                load_sem.at[2 * f + h]))
    for k, (src, dst) in enumerate(((m_in, mac), (wy_in, wy), (wz_in, wz), (py_in, py), (pz_in, pz))):
        loads.append(pltpu.make_async_copy(src, dst, load_sem.at[4 + k]))
    loads[4].start()
    for copy in loads[:4] + loads[5:]:
        copy.start()

    lane = lax.broadcasted_iota(jnp.int32, (8, LANES), 1)
    first, last = lane == 0, lane == LANES - 1
    first2, last2 = lane < 2, lane >= LANES - 2

    loads[4].wait()
    lane4 = lax.broadcasted_iota(jnp.int32, (4, LANES), 1)
    zone = lane4 // 32
    layers = [mac[pl.ds(z, 4, stride=4), :] for z in range(4)]
    for dest in range(16):
        parts = [pltpu.roll(layers[z], (32 * z - 8 * dest + 1) % LANES, 1) for z in range(4)]
        tile = jnp.where(zone == 0, parts[0], jnp.where(zone == 1, parts[1], jnp.where(zone == 2, parts[2], parts[3])))
        s1[pl.ds(8 * dest, 4), :] = tile

    for copy in loads[:4]:
        copy.wait()
    pl.semaphore_wait(barrier, len(peers))

    x_copies, y_copies, d_copies = [], [], []
    lo, hi = pl.ds(M, M), pl.ds(BX, M)
    before, after = pl.ds(0, M), pl.ds(M + BX, M)
    row_lo, row_hi = pl.ds(RY, M), pl.ds(RY + BY - M, M)
    row_before, row_after = pl.ds(RY - M, M), pl.ds(RY + BY, M)
    rows, planes = pl.ds(RY, BY), pl.ds(M, BX)

    def remote(src, dst, send, recv, peer):
        return pltpu.make_async_remote_copy(
            src_ref=src, dst_ref=dst, send_sem=send, recv_sem=recv, device_id=peer, device_id_type=MESH)

    for k, (src, dst, peer) in enumerate(((hi, before, (up_x, b)), (lo, after, (down_x, b)))):
        x_copies.append(remote(pc0.at[:, :, src, rows, :], pc0.at[:, :, dst, rows, :], x_send.at[k], x_recv.at[k], peer))
    for k, (src, dst, peer) in enumerate(((row_hi, row_before, (a, up_y)), (row_lo, row_after, (a, down_y)))):
        y_copies.append(remote(pc0.at[:, :, planes, src, :], pc0.at[:, :, planes, dst, :], y_send.at[k], y_recv.at[k], peer))
    first3, last3, before3, after3 = pl.ds(M, 3), pl.ds(BX + 1, 3), pl.ds(1, 3), pl.ds(M + BX, 3)
    rows_lo, rows_hi, rows_before, rows_after = pl.ds(RY, 3), pl.ds(RY + BY - 3, 3), pl.ds(RY - 3, 3), pl.ds(RY + BY, 3)
    for k, (sx, dx, sy, dy, peer) in enumerate((
        (last3, before3, rows_hi, rows_before, corners[0]),
        (last3, before3, rows_lo, rows_after, corners[1]),
        (first3, after3, rows_hi, rows_before, corners[2]),
        (first3, after3, rows_lo, rows_after, corners[3]),
    )):
        d_copies.append(remote(pc0.at[:, :, sx, sy, :], pc0.at[:, :, dx, dy, :], d_send.at[k], d_recv.at[k], peer))

    def exchange(src, dst, send, recv, size):
        out = []
        for k, to in enumerate(others):
            out.append(remote(
                src.at[pl.ds(pl.multiple_of(8 * to, 8), size), :], dst.at[pl.ds(pl.multiple_of(8 * b, 8), size), :],
                send.at[k], recv.at[k], (a, to)))
        return out

    here = pl.ds(pl.multiple_of(8 * b, 8), 4)
    t_copies = exchange(s1, r1, t_send, t_recv, 4)
    for copy in t_copies + y_copies + x_copies + d_copies:
        copy.start()
    r1[here, :] = s1[here, :]
    def flux(p, planes_):
        tiles = [(e, pl.ds(r, 8), r) for e in planes_ for r in ROWS]
        for e, at, r in tiles:
            v = [p[0, h, e, at, :] for h in range(2)]
            fwd = [pltpu.roll(v[h], 1, 1) for h in range(2)]
            bwd = [pltpu.roll(v[h], LANES - 1, 1) for h in range(2)]
            fz[0, e, at, :] = jnp.where(last, bwd[1], bwd[0]) - jnp.where(first, v[0], fwd[0])
            fz[1, e, at, :] = jnp.where(last, v[1], bwd[1]) - jnp.where(first, fwd[0], fwd[1])
        for e, at, r in tiles:
            for h in range(2):
                gx = p[0, h, e + 1, at, :] - p[0, h, e - 1, at, :]
                gy = p[0, h, e, pl.ds(r + 1, 8), :] - p[0, h, e, pl.ds(r - 1, 8), :]
                sx, sy = gx * gx, gy * gy
                total = sx + sy
                planar = total + 4.0
                ratio = (total * total - 8.0 * (sx * sy)) / (planar * planar)
                factor = ROOT + (0.3 * ROOT) * ratio
                stiff = factor * factor
                fx[h, e, at, :] = stiff * gx
                fy[h, e, at, :] = stiff * gy
                fz[h, e, at, :] = stiff * fz[h, e, at, :]
        for e, at, r in tiles:
            w = [fz[h, e, at, :] for h in range(2)]
            fwd = [pltpu.roll(w[h], 1, 1) for h in range(2)]
            bwd = [pltpu.roll(w[h], LANES - 1, 1) for h in range(2)]
            fz[0, e, at, :] = jnp.where(last, bwd[1], bwd[0]) - jnp.where(first, 0.0, fwd[0])
            fz[1, e, at, :] = jnp.where(last, 0.0, bwd[1]) - jnp.where(first, fwd[0], fwd[1])

    def new_phase(pc, h, e, r, theta):
        at = pl.ds(r, 8)
        div = (fx[h, e + 1, at, :] - fx[h, e - 1, at, :]
               + (fy[h, e, pl.ds(r + 1, 8), :] - fy[h, e, pl.ds(r - 1, 8), :]) + fz[h, e, at, :])
        old, conc = pc[0, h, e, at, :], pc[1, h, e, at, :]
        square = 1.0 - old * old
        step = square * (0.1 * old - 0.2 * (square * (theta + conc))) + div
        return old + step, step

    def new_solute(pc, e, r, steps):
        at = pl.ds(r, 8)
        v = [pc[1, h, e, at, :] for h in range(2)]
        fwd = [pltpu.roll(v[h], 2, 1) for h in range(2)]
        bwd = [pltpu.roll(v[h], LANES - 2, 1) for h in range(2)]
        head = jnp.where(first, v[0], pltpu.roll(v[0], 1, 1))
        tail = jnp.where(last, v[1], pltpu.roll(v[1], LANES - 1, 1))
        lz = [jnp.where(last2, bwd[1], bwd[0]) + jnp.where(first2, head, fwd[0]),
              jnp.where(last2, tail, bwd[1]) + jnp.where(first2, fwd[0], fwd[1])]
        out = []
        for h in range(2):
            lap = (pc[1, h, e + 2, at, :] + pc[1, h, e - 2, at, :]
                   + (pc[1, h, e, pl.ds(r + 2, 8), :] + pc[1, h, e, pl.ds(r - 2, 8), :]) + lz[h])
            out.append(0.85 * v[h] + (0.025 * lap + 0.5 * steps[h]))
        return out

    def flux_planes(p, start, gap, count):
        def run(i, carry):
            flux(p, [start + gap * i + q for q in range(count)])
            return carry
        return run

    def first_update(group):
        e0 = 4 * group + 2
        for r in ROWS:
            at = pl.ds(r, 8)
            low = [th[group, h, at, :] for h in range(2)]
            rise = [th[group + 1, h, at, :] - low[h] for h in range(2)]
            for q in range(4):
                steps = []
                for h in range(2):
                    new, step = new_phase(pc0, h, e0 + q, r, low[h] + (0.125 + 0.25 * q) * rise[h])
                    pc1[0, h, e0 + q, at, :] = new
                    steps.append(step)
                for h, new in enumerate(new_solute(pc0, e0 + q, r, steps)):
                    pc1[1, h, e0 + q, at, :] = new

    def second_update(group, with_solute):
        e0 = 4 * group + 4
        for r in OWN:
            at = pl.ds(r, 8)
            to = pl.ds(r - RY, 8)
            total = [None, None]
            for q in range(4):
                frac = 0.125 + 0.25 * ((q + 2) % 4)
                steps = []
                for h in range(2):
                    low = th[group + q // 2, h, at, :]
                    new, step = new_phase(pc1, h, e0 + q, r, low + frac * (th[group + q // 2 + 1, h, at, :] - low))
                    out[0, h, e0 + q - M, to, :] = new
                    change = new - pc0[0, h, e0 + q, at, :]
                    total[h] = change if total[h] is None else total[h] + change
                    steps.append(step)
                if with_solute:
                    for h, new in enumerate(new_solute(pc1, e0 + q, r, steps)):
                        out[1, h, e0 + q - M, to, :] = new
            for h in range(2):
                lat[pl.ds(pl.multiple_of(BY * group + r - RY, 8), 8), pl.ds(h * LANES, LANES)] = total[h]

        rows_y = lat[pl.ds(pl.multiple_of(BY * group, BY), BY), :]
        oy[pl.ds(pl.multiple_of(8 * group, 8), 8), :] = jnp.dot(py[...], three(rows_y, 0), preferred_element_type=jnp.float32)[:8]

    def late_solute(group):
        e0 = 4 * group + 4
        for r in OWN:
            to = pl.ds(r - RY, 8)
            for q in range(4):
                steps = [out[0, h, e0 + q - M, to, :] - pc1[0, h, e0 + q, pl.ds(r, 8), :] for h in range(2)]
                for h, new in enumerate(new_solute(pc1, e0 + q, r, steps)):
                    out[1, h, e0 + q - M, to, :] = new

    for copy in y_copies:
        copy.wait_recv()
    lax.fori_loop(0, 2, flux_planes(pc0, 5, 7, 7), 0)
    for copy in t_copies:
        copy.wait_recv()
    xs[0] = r1[pl.ds(3, 16, stride=8), :]
    xs[1] = r1[pl.ds(0, 16, stride=8), :]
    h_copies = [remote(xs.at[0], xr.at[0], h_send.at[0], h_recv.at[0], (up_x, b)),
                remote(xs.at[1], xr.at[1], h_send.at[1], h_recv.at[1], (down_x, b))]
    for copy in h_copies:
        copy.start()


    for copy in loads[5:]:
        copy.wait()

    def temperature(first_x, coarse):
        count = len(coarse)
        on_rows = jnp.dot(three(jnp.concatenate(coarse, axis=0), 1), wy[...], preferred_element_type=jnp.float32)
        parts = []
        for x in range(count):
            part = jnp.concatenate([on_rows[16 * x:16 * x + 16, LANES * z:LANES * z + LANES] for z in range(4)], axis=0)
            parts.append(jnp.transpose(part)[:40])
        full = jnp.dot(three(jnp.concatenate(parts, axis=0), 1), wz[...], preferred_element_type=jnp.float32)
        for x in range(count):
            for h in range(2):
                th[first_x[x], h, pl.ds(4, 40), :] = full[40 * x:40 * x + 40, LANES * h:LANES * h + LANES]

    temperature((1, 2, 3, 4), [r1[pl.ds(x, 16, stride=8), :] for x in range(4)])
    lax.fori_loop(1, 4, lambda i, carry: (first_update(i), carry)[1], 0)
    lax.fori_loop(0, 2, flux_planes(pc1, 7, 5, 5), 0)
    lax.fori_loop(1, 3, lambda i, carry: (second_update(i, True), carry)[1], 0)

    for side in (1, 0):
        for copy in [x_copies[side]] + d_copies[2 * side:2 * side + 2]:
            copy.wait_recv()
        flux(pc0, [(1, 19)[side] + q for q in range(4)])
        h_copies[side].wait_recv()
        temperature(((0,), (5,))[side], [xr[side]])
        first_update((0, 4)[side])
        flux(pc1, [(3, 17)[side] + q for q in range(4)])
        second_update((0, 3)[side], False)

    on_z = lax.dot_general(pz[...], three(oy[...], 1), (((1,), (1,)), ((), ())), preferred_element_type=jnp.float32)
    s2[pl.ds(0, 16, stride=8), :] = jnp.concatenate([on_z[16 * z:16 * z + 16] for z in range(4)], axis=1)
    l_copies = exchange(s2, r2, l_send, l_recv, 1)
    for copy in l_copies:
        copy.start()
    r2[pl.ds(pl.multiple_of(8 * b, 8), 1), :] = s2[pl.ds(pl.multiple_of(8 * b, 8), 1), :]
    lax.fori_loop(0, 2, lambda i, carry: (late_solute(3 * i), carry)[1], 0)
    for copy in l_copies:
        copy.wait_recv()
    sources = r2[pl.ds(0, 16, stride=8), :]
    ahead = lax.broadcasted_iota(jnp.int32, (16, LANES), 1) // 8 - lax.broadcasted_iota(jnp.int32, (16, LANES), 0)
    result = sources
    for d in range(1, 16):
        moved = pltpu.roll(pltpu.roll(sources, 8 * d, 1), 16 - d, 0)
        result = jnp.where((ahead == d) | (ahead == d - 16), moved, result)
    for z in range(4):
        lat_v[pl.ds(z, 4, stride=4), :] = result[4 * z:4 * z + 4]

    for copy in x_copies + y_copies + d_copies + t_copies + h_copies + l_copies:
        copy.wait_send()


def store_kernel(field, lat, p_out, c_out, lat_out, sem):
    copies = [pltpu.make_async_copy(lat, lat_out, sem.at[4])]
    for f, dst in enumerate((p_out, c_out)):
        for h in range(2):
            copies.append(pltpu.make_async_copy(field.at[f, h], dst.at[:, :, pl.ds(h * LANES, LANES)], sem.at[2 * f + h]))
    for copy in copies:
        copy.start()
    for copy in copies:
        copy.wait()


def body(nx, ny, phase, solute, macro_temp):
    macro = jnp.transpose(macro_temp, (0, 2, 1)).reshape(16, LANES)
    weights = tables()
    f32 = jnp.float32
    anywhere = pl.BlockSpec(memory_space=pl.ANY)
    here = pl.BlockSpec(memory_space=pltpu.VMEM)
    wide = pltpu.VMEM((2, EX, EY, LANES), f32)
    both = pltpu.VMEM((2, 2, EX, EY, LANES), f32)
    dma = pltpu.SemaphoreType.DMA
    field, latent = pl.pallas_call(
        functools.partial(kernel, nx, ny),
        out_shape=(pltpu.VMEM((2, 2, BX, BY, LANES), f32), pltpu.VMEM((16, LANES), f32)),
        in_specs=[anywhere] * 7,
        out_specs=(here, here),
        scratch_shapes=[both] * 2 + [wide] * 3 + [
            pltpu.VMEM((6, 2, EY, LANES), f32),
            pltpu.VMEM((4 * BY, 2 * LANES), f32), pltpu.VMEM((32, 2 * LANES), f32)] + [
            pltpu.VMEM(w.shape, w.dtype) for w in weights] + [
            pltpu.VMEM((16, LANES), f32),
            pltpu.VMEM((128, LANES), f32), pltpu.VMEM((128, LANES), f32),
            pltpu.VMEM((2, 16, LANES), f32), pltpu.VMEM((2, 16, LANES), f32),
            pltpu.VMEM((128, LANES), f32), pltpu.VMEM((128, LANES), f32),
            dma((9,)), dma((2,)), dma((2,)), dma((2,)), dma((2,)), dma((4,)), dma((4,)),
            dma((16,)), dma((16,)), dma((2,)), dma((2,)), dma((16,)), dma((16,)),
        ],
        compiler_params=pltpu.CompilerParams(collective_id=0, has_side_effects=True, vmem_limit_bytes=60 << 20),
        name="substeps",
    )(phase, solute, macro, *weights)
    new_phase, new_solute, latent = pl.pallas_call(
        store_kernel,
        out_shape=(jax.ShapeDtypeStruct(phase.shape, f32), jax.ShapeDtypeStruct(solute.shape, f32),
                   jax.ShapeDtypeStruct((16, LANES), f32)),
        in_specs=[anywhere] * 2,
        out_specs=(anywhere,) * 3,
        scratch_shapes=[dma((5,))],
        compiler_params=pltpu.CompilerParams(vmem_limit_bytes=1 << 20),
        name="store",
    )(field, latent)
    return new_phase, new_solute, jnp.transpose(latent.reshape(4, 4, LANES), (0, 2, 1))


def solution(mesh):
    in_specs = (P("gx", "gy", None), P("gx", "gy", None), P("gx", None, "gy"))
    out_specs = (P("gx", "gy", None), P("gx", "gy", None), P("gx", None, "gy"))
    return jax.shard_map(
        functools.partial(body, mesh.shape["gx"], mesh.shape["gy"]),
        mesh=mesh, in_specs=in_specs, out_specs=out_specs, check_vma=False)
```

```python
import functools

import jax
import jax.numpy as jnp
import numpy as np
from jax import lax
from jax.experimental import pallas as pl
from jax.experimental.pallas import tpu as pltpu
from jax.sharding import PartitionSpec as P

MESH = pl.DeviceIdType.MESH

BX, BY = 16, 32
M = 4
EX = BX + 2 * M
RY = 8
EY = 48
LANES = 128
ROOT = 0.025 ** 0.5
ROWS = (4, 12, 20, 28, 36)
OWN = (8, 16, 24, 32)


def tables():
    wy = np.zeros((128, 4 * LANES), np.float32)
    for row in range(40):
        y = row - 4
        low = (2 * y - 3) // 8
        frac = (2 * y - 3 - 8 * low) / 8.0
        for hit, weight in ((low + 1, 1.0 - frac), (low + 2, frac)):
            if 0 <= hit < 10:
                for z in range(4):
                    wy[32 * z + hit, LANES * z + row] += weight
    wz = np.zeros((64, 256), np.float32)
    for fine in range(256):
        low = (2 * fine - 3) // 8
        frac = (2 * fine - 3 - 8 * low) / 8.0
        for hit, weight in ((low, 1.0 - frac), (low + 1, frac)):
            hit = min(max(hit, 0), 63)
            wz[16 * (hit % 4) + hit // 4, fine] += weight
    py = np.zeros((16, BY), np.float32)
    for row in range(BY):
        py[row // 4, row] = 1.0
    pz = np.zeros((64, 256), np.float32)
    for fine in range(256):
        z = fine // 4
        pz[16 * (z % 4) + z // 4, fine] = 1.0 / 128.0
    tall = [np.concatenate([t] * 3, axis=0) for t in (wy, wz)]
    wide = [np.concatenate([t] * 3, axis=1) for t in (py, pz)]
    return [jnp.asarray(t, jnp.bfloat16) for t in tall + wide]


def three(value, axis):
    high = value.astype(jnp.bfloat16)
    rest = value - high.astype(jnp.float32)
    middle = rest.astype(jnp.bfloat16)
    low = (rest - middle.astype(jnp.float32)).astype(jnp.bfloat16)
    return jnp.concatenate([high, middle, low], axis=axis)


def kernel(nx, ny, p_in, c_in, m_in, wy_in, wz_in, py_in, pz_in, out, lat_v,
           pc0, pc1, fx, fy, fz, th, lat, oy, wy, wz, py, pz, mac, s1, r1, xs, xr, s2, r2,
           load_sem, x_send, x_recv, y_send, y_recv, d_send, d_recv, t_send, t_recv, h_send, h_recv, l_send, l_recv):
    a = lax.axis_index("gx")
    b = lax.axis_index("gy")
    up_x, down_x = lax.rem(a + 1, nx), lax.rem(a + nx - 1, nx)
    up_y, down_y = lax.rem(b + 1, ny), lax.rem(b + ny - 1, ny)

    barrier = pltpu.get_barrier_semaphore()
    corners = ((up_x, up_y), (up_x, down_y), (down_x, up_y), (down_x, down_y))
    far, near, core = b // 8, (b // 2) % 4, b % 2
    steps = [(df, dn, dc) for df in (1, 0) for dn in (2, 1, 3, 0) for dc in (0, 1)][:-2] + [(0, 0, 1)]
    steps.sort(key=lambda d: -(2 * d[0] + min(d[1], 4 - d[1])))
    others = [((far + df) % 2) * 8 + ((near + dn) % 4) * 2 + (core + dc) % 2 for df, dn, dc in steps]
    peers = [(a, to) for to in others[:12]] + list(corners) + [(up_x, b), (down_x, b)] + [(a, to) for to in others[12:]]
    for peer in peers:
        pl.semaphore_signal(barrier, inc=1, device_id=peer, device_id_type=MESH)

    loads = []
    for f, src in enumerate((p_in, c_in)):
        for h in range(2):
            loads.append(pltpu.make_async_copy(
                src.at[:, :, pl.ds(h * LANES, LANES)],
                pc0.at[f, h, pl.ds(M, BX), pl.ds(RY, BY), :],
                load_sem.at[2 * f + h]))
    for k, (src, dst) in enumerate(((m_in, mac), (wy_in, wy), (wz_in, wz), (py_in, py), (pz_in, pz))):
        loads.append(pltpu.make_async_copy(src, dst, load_sem.at[4 + k]))
    loads[4].start()
    for copy in loads[:4] + loads[5:]:
        copy.start()

    lane = lax.broadcasted_iota(jnp.int32, (8, LANES), 1)
    first, last = lane == 0, lane == LANES - 1
    first2, last2 = lane < 2, lane >= LANES - 2

    loads[4].wait()
    lane4 = lax.broadcasted_iota(jnp.int32, (4, LANES), 1)
    zone = lane4 // 32
    layers = [mac[pl.ds(z, 4, stride=4), :] for z in range(4)]
    for dest in range(16):
        parts = [pltpu.roll(layers[z], (32 * z - 8 * dest + 1) % LANES, 1) for z in range(4)]
        tile = jnp.where(zone == 0, parts[0], jnp.where(zone == 1, parts[1], jnp.where(zone == 2, parts[2], parts[3])))
        s1[pl.ds(8 * dest, 4), :] = tile

    for copy in loads[:4]:
        copy.wait()
    pl.semaphore_wait(barrier, len(peers))

    x_copies, y_copies, d_copies = [], [], []
    lo, hi = pl.ds(M, M), pl.ds(BX, M)
    before, after = pl.ds(0, M), pl.ds(M + BX, M)
    row_lo, row_hi = pl.ds(RY, M), pl.ds(RY + BY - M, M)
    row_before, row_after = pl.ds(RY - M, M), pl.ds(RY + BY, M)
    rows, planes = pl.ds(RY, BY), pl.ds(M, BX)

    def remote(src, dst, send, recv, peer):
        return pltpu.make_async_remote_copy(
            src_ref=src, dst_ref=dst, send_sem=send, recv_sem=recv, device_id=peer, device_id_type=MESH)

    for k, (src, dst, peer) in enumerate(((hi, before, (up_x, b)), (lo, after, (down_x, b)))):
        x_copies.append(remote(pc0.at[:, :, src, rows, :], pc0.at[:, :, dst, rows, :], x_send.at[k], x_recv.at[k], peer))
    for k, (src, dst, peer) in enumerate(((row_hi, row_before, (a, up_y)), (row_lo, row_after, (a, down_y)))):
        y_copies.append(remote(pc0.at[:, :, planes, src, :], pc0.at[:, :, planes, dst, :], y_send.at[k], y_recv.at[k], peer))
    for f, n in ((0, 3), (1, 2)):
        low_x, high_x, before_x, after_x = pl.ds(M, n), pl.ds(M + BX - n, n), pl.ds(M - n, n), pl.ds(M + BX, n)
        low_y, high_y, before_y, after_y = pl.ds(RY, n), pl.ds(RY + BY - n, n), pl.ds(RY - n, n), pl.ds(RY + BY, n)
        for k, (sx, dx, sy, dy, peer) in enumerate((
            (high_x, before_x, high_y, before_y, corners[0]),
            (high_x, before_x, low_y, after_y, corners[1]),
            (low_x, after_x, high_y, before_y, corners[2]),
            (low_x, after_x, low_y, after_y, corners[3]),
        )):
            d_copies.append(remote(
                pc0.at[f, :, sx, sy, :], pc0.at[f, :, dx, dy, :], d_send.at[4 * f + k], d_recv.at[4 * f + k], peer))

    def exchange(src, dst, send, recv, size):
        out = []
        for k, to in enumerate(others):
            out.append(remote(
                src.at[pl.ds(pl.multiple_of(8 * to, 8), size), :], dst.at[pl.ds(pl.multiple_of(8 * b, 8), size), :],
                send.at[k], recv.at[k], (a, to)))
        return out

    here = pl.ds(pl.multiple_of(8 * b, 8), 4)
    t_copies = exchange(s1, r1, t_send, t_recv, 4)
    for copy in t_copies + y_copies + x_copies[::-1] + d_copies:
        copy.start()
    r1[here, :] = s1[here, :]
    def flux(p, planes_):
        tiles = [(e, pl.ds(r, 8), r) for e in planes_ for r in ROWS]
        for e, at, r in tiles:
            v = [p[0, h, e, at, :] for h in range(2)]
            fwd = [pltpu.roll(v[h], 1, 1) for h in range(2)]
            bwd = [pltpu.roll(v[h], LANES - 1, 1) for h in range(2)]
            fz[0, e, at, :] = jnp.where(last, bwd[1], bwd[0]) - jnp.where(first, v[0], fwd[0])
            fz[1, e, at, :] = jnp.where(last, v[1], bwd[1]) - jnp.where(first, fwd[0], fwd[1])
        for e, at, r in tiles:
            for h in range(2):
                gx = p[0, h, e + 1, at, :] - p[0, h, e - 1, at, :]
                gy = p[0, h, e, pl.ds(r + 1, 8), :] - p[0, h, e, pl.ds(r - 1, 8), :]
                sx, sy = gx * gx, gy * gy
                total = sx + sy
                planar = total + 4.0
                ratio = (total * total - 8.0 * (sx * sy)) / (planar * planar)
                factor = ROOT + (0.3 * ROOT) * ratio
                stiff = factor * factor
                fx[h, e, at, :] = stiff * gx
                fy[h, e, at, :] = stiff * gy
                fz[h, e, at, :] = stiff * fz[h, e, at, :]
        for e, at, r in tiles:
            w = [fz[h, e, at, :] for h in range(2)]
            fwd = [pltpu.roll(w[h], 1, 1) for h in range(2)]
            bwd = [pltpu.roll(w[h], LANES - 1, 1) for h in range(2)]
            fz[0, e, at, :] = jnp.where(last, bwd[1], bwd[0]) - jnp.where(first, 0.0, fwd[0])
            fz[1, e, at, :] = jnp.where(last, 0.0, bwd[1]) - jnp.where(first, fwd[0], fwd[1])

    def new_phase(pc, h, e, r, theta):
        at = pl.ds(r, 8)
        div = (fx[h, e + 1, at, :] - fx[h, e - 1, at, :]
               + (fy[h, e, pl.ds(r + 1, 8), :] - fy[h, e, pl.ds(r - 1, 8), :]) + fz[h, e, at, :])
        old, conc = pc[0, h, e, at, :], pc[1, h, e, at, :]
        square = 1.0 - old * old
        step = square * (0.1 * old - 0.2 * (square * (theta + conc))) + div
        return old + step, step

    def new_solute(pc, e, r, steps):
        at = pl.ds(r, 8)
        v = [pc[1, h, e, at, :] for h in range(2)]
        fwd = [pltpu.roll(v[h], 2, 1) for h in range(2)]
        bwd = [pltpu.roll(v[h], LANES - 2, 1) for h in range(2)]
        head = jnp.where(first, v[0], pltpu.roll(v[0], 1, 1))
        tail = jnp.where(last, v[1], pltpu.roll(v[1], LANES - 1, 1))
        lz = [jnp.where(last2, bwd[1], bwd[0]) + jnp.where(first2, head, fwd[0]),
              jnp.where(last2, tail, bwd[1]) + jnp.where(first2, fwd[0], fwd[1])]
        out = []
        for h in range(2):
            lap = (pc[1, h, e + 2, at, :] + pc[1, h, e - 2, at, :]
                   + (pc[1, h, e, pl.ds(r + 2, 8), :] + pc[1, h, e, pl.ds(r - 2, 8), :]) + lz[h])
            out.append(0.85 * v[h] + (0.025 * lap + 0.5 * steps[h]))
        return out

    def flux_planes(p, start, gap, count):
        def run(i, carry):
            flux(p, [start + gap * i + q for q in range(count)])
            return carry
        return run

    def first_update(group):
        e0 = 4 * group + 2
        for r in ROWS:
            at = pl.ds(r, 8)
            low = [th[group, h, at, :] for h in range(2)]
            rise = [th[group + 1, h, at, :] - low[h] for h in range(2)]
            for q in range(4):
                steps = []
                for h in range(2):
                    new, step = new_phase(pc0, h, e0 + q, r, low[h] + (0.125 + 0.25 * q) * rise[h])
                    pc1[0, h, e0 + q, at, :] = new
                    steps.append(step)
                for h, new in enumerate(new_solute(pc0, e0 + q, r, steps)):
                    pc1[1, h, e0 + q, at, :] = new

    def second_update(group, with_solute):
        e0 = 4 * group + 4
        for r in OWN:
            at = pl.ds(r, 8)
            to = pl.ds(r - RY, 8)
            total = [None, None]
            for q in range(4):
                frac = 0.125 + 0.25 * ((q + 2) % 4)
                steps = []
                for h in range(2):
                    low = th[group + q // 2, h, at, :]
                    new, step = new_phase(pc1, h, e0 + q, r, low + frac * (th[group + q // 2 + 1, h, at, :] - low))
                    out[0, h, e0 + q - M, to, :] = new
                    change = new - pc0[0, h, e0 + q, at, :]
                    total[h] = change if total[h] is None else total[h] + change
                    steps.append(step)
                if with_solute:
                    for h, new in enumerate(new_solute(pc1, e0 + q, r, steps)):
                        out[1, h, e0 + q - M, to, :] = new
            for h in range(2):
                lat[pl.ds(pl.multiple_of(BY * group + r - RY, 8), 8), pl.ds(h * LANES, LANES)] = total[h]

        rows_y = lat[pl.ds(pl.multiple_of(BY * group, BY), BY), :]
        oy[pl.ds(pl.multiple_of(8 * group, 8), 8), :] = jnp.dot(py[...], three(rows_y, 0), preferred_element_type=jnp.float32)[:8]

    def late_solute(group):
        e0 = 4 * group + 4
        for r in OWN:
            to = pl.ds(r - RY, 8)
            for q in range(4):
                steps = [out[0, h, e0 + q - M, to, :] - pc1[0, h, e0 + q, pl.ds(r, 8), :] for h in range(2)]
                for h, new in enumerate(new_solute(pc1, e0 + q, r, steps)):
                    out[1, h, e0 + q - M, to, :] = new

    for copy in y_copies:
        copy.wait_recv()
    lax.fori_loop(0, 2, flux_planes(pc0, 5, 7, 7), 0)
    for copy in t_copies:
        copy.wait_recv()
    xs[0] = r1[pl.ds(3, 16, stride=8), :]
    xs[1] = r1[pl.ds(0, 16, stride=8), :]
    h_copies = [remote(xs.at[0], xr.at[0], h_send.at[0], h_recv.at[0], (up_x, b)),
                remote(xs.at[1], xr.at[1], h_send.at[1], h_recv.at[1], (down_x, b))]
    for copy in h_copies:
        copy.start()


    for copy in loads[5:]:
        copy.wait()

    def temperature(first_x, coarse):
        count = len(coarse)
        on_rows = jnp.dot(three(jnp.concatenate(coarse, axis=0), 1), wy[...], preferred_element_type=jnp.float32)
        parts = []
        for x in range(count):
            part = jnp.concatenate([on_rows[16 * x:16 * x + 16, LANES * z:LANES * z + LANES] for z in range(4)], axis=0)
            parts.append(jnp.transpose(part)[:40])
        full = jnp.dot(three(jnp.concatenate(parts, axis=0), 1), wz[...], preferred_element_type=jnp.float32)
        for x in range(count):
            for h in range(2):
                th[first_x[x], h, pl.ds(4, 40), :] = full[40 * x:40 * x + 40, LANES * h:LANES * h + LANES]

    temperature((1, 2, 3, 4), [r1[pl.ds(x, 16, stride=8), :] for x in range(4)])
    lax.fori_loop(1, 4, lambda i, carry: (first_update(i), carry)[1], 0)
    lax.fori_loop(0, 2, flux_planes(pc1, 7, 5, 5), 0)
    lax.fori_loop(1, 3, lambda i, carry: (second_update(i, True), carry)[1], 0)

    for side in (1, 0):
        for copy in [x_copies[side]] + d_copies[2 * side:2 * side + 2] + d_copies[4 + 2 * side:6 + 2 * side]:
            copy.wait_recv()
        flux(pc0, [(1, 19)[side] + q for q in range(4)])
        h_copies[side].wait_recv()
        temperature(((0,), (5,))[side], [xr[side]])
        first_update((0, 4)[side])
        flux(pc1, [(3, 17)[side] + q for q in range(4)])
        second_update((0, 3)[side], False)

    on_z = lax.dot_general(pz[...], three(oy[...], 1), (((1,), (1,)), ((), ())), preferred_element_type=jnp.float32)
    s2[pl.ds(0, 16, stride=8), :] = jnp.concatenate([on_z[16 * z:16 * z + 16] for z in range(4)], axis=1)
    l_copies = exchange(s2, r2, l_send, l_recv, 1)
    for copy in l_copies:
        copy.start()
    r2[pl.ds(pl.multiple_of(8 * b, 8), 1), :] = s2[pl.ds(pl.multiple_of(8 * b, 8), 1), :]
    lax.fori_loop(0, 2, lambda i, carry: (late_solute(3 * i), carry)[1], 0)
    for copy in l_copies:
        copy.wait_recv()
    sources = r2[pl.ds(0, 16, stride=8), :]
    ahead = lax.broadcasted_iota(jnp.int32, (16, LANES), 1) // 8 - lax.broadcasted_iota(jnp.int32, (16, LANES), 0)
    result = sources
    for d in range(1, 16):
        moved = pltpu.roll(pltpu.roll(sources, 8 * d, 1), 16 - d, 0)
        result = jnp.where((ahead == d) | (ahead == d - 16), moved, result)
    for z in range(4):
        lat_v[pl.ds(z, 4, stride=4), :] = result[4 * z:4 * z + 4]

    for copy in x_copies + y_copies + d_copies + t_copies + h_copies + l_copies:
        copy.wait_send()


def store_kernel(field, lat, p_out, c_out, lat_out, sem):
    copies = [pltpu.make_async_copy(lat, lat_out, sem.at[4])]
    for f, dst in enumerate((p_out, c_out)):
        for h in range(2):
            copies.append(pltpu.make_async_copy(field.at[f, h], dst.at[:, :, pl.ds(h * LANES, LANES)], sem.at[2 * f + h]))
    for copy in copies:
        copy.start()
    for copy in copies:
        copy.wait()


def body(nx, ny, phase, solute, macro_temp):
    macro = jnp.transpose(macro_temp, (0, 2, 1)).reshape(16, LANES)
    weights = tables()
    f32 = jnp.float32
    anywhere = pl.BlockSpec(memory_space=pl.ANY)
    here = pl.BlockSpec(memory_space=pltpu.VMEM)
    wide = pltpu.VMEM((2, EX, EY, LANES), f32)
    both = pltpu.VMEM((2, 2, EX, EY, LANES), f32)
    dma = pltpu.SemaphoreType.DMA
    field, latent = pl.pallas_call(
        functools.partial(kernel, nx, ny),
        out_shape=(pltpu.VMEM((2, 2, BX, BY, LANES), f32), pltpu.VMEM((16, LANES), f32)),
        in_specs=[anywhere] * 7,
        out_specs=(here, here),
        scratch_shapes=[both] * 2 + [wide] * 3 + [
            pltpu.VMEM((6, 2, EY, LANES), f32),
            pltpu.VMEM((4 * BY, 2 * LANES), f32), pltpu.VMEM((32, 2 * LANES), f32)] + [
            pltpu.VMEM(w.shape, w.dtype) for w in weights] + [
            pltpu.VMEM((16, LANES), f32),
            pltpu.VMEM((128, LANES), f32), pltpu.VMEM((128, LANES), f32),
            pltpu.VMEM((2, 16, LANES), f32), pltpu.VMEM((2, 16, LANES), f32),
            pltpu.VMEM((128, LANES), f32), pltpu.VMEM((128, LANES), f32),
            dma((9,)), dma((2,)), dma((2,)), dma((2,)), dma((2,)), dma((8,)), dma((8,)),
            dma((16,)), dma((16,)), dma((2,)), dma((2,)), dma((16,)), dma((16,)),
        ],
        compiler_params=pltpu.CompilerParams(collective_id=0, has_side_effects=True, vmem_limit_bytes=60 << 20),
        name="substeps",
    )(phase, solute, macro, *weights)
    new_phase, new_solute, latent = pl.pallas_call(
        store_kernel,
        out_shape=(jax.ShapeDtypeStruct(phase.shape, f32), jax.ShapeDtypeStruct(solute.shape, f32),
                   jax.ShapeDtypeStruct((16, LANES), f32)),
        in_specs=[anywhere] * 2,
        out_specs=(anywhere,) * 3,
        scratch_shapes=[dma((5,))],
        compiler_params=pltpu.CompilerParams(vmem_limit_bytes=1 << 20),
        name="store",
    )(field, latent)
    return new_phase, new_solute, jnp.transpose(latent.reshape(4, 4, LANES), (0, 2, 1))


def solution(mesh):
    in_specs = (P("gx", "gy", None), P("gx", "gy", None), P("gx", None, "gy"))
    out_specs = (P("gx", "gy", None), P("gx", "gy", None), P("gx", None, "gy"))
    return jax.shard_map(
        functools.partial(body, mesh.shape["gx"], mesh.shape["gy"]),
        mesh=mesh, in_specs=in_specs, out_specs=out_specs, check_vma=False)
```
